32 devices in a mesh: grp: 2 (over x), scan: 8 (over z, y), det: 2 (over core).
Axes of the slice: x: 2, y: 2, z: 4, core: 2. Of those that a mesh axis runs over, the one named last changes fastest.
Arguments:
- spectra: float32 [16384, 4096], P(('grp', 'scan'), 'det'), parts along dimension 0, may hold values from 0 to 544, as said below
- basis: float32 [64, 4096], P('grp', 'det'), parts along dimension 0, may hold values from 0.03 to 8, as said below
- loadings: float32 [64, 8192], P('grp', 'scan'), parts along dimension 0, may hold values from 0.005 to 6, as said below
Outputs:
- new_loadings: float32 [64, 8192], P('grp', 'scan'), parts along dimension 0
- new_basis: float32 [64, 4096], P('grp', 'det'), parts along dimension 0
The draws below stay inside these ranges and needn't reach their ends.
There are 2 independent parts, one for each index of `grp`. The reference program is written for one: setup_inputs(seed, part) draws one part's arguments, and reference() takes and returns one part's arrays. A program takes and returns all parts, laid end to end along the dimension named above; each array names one. Nothing has to cross between parts.
Inputs may be any that keep to these rules, and one draw needn't show every extreme that they name: `spectra`: intensities are nonnegative. `basis`: entries are positive. `loadings`: entries are positive.
All inputs are finite; a program needn't handle non-finite values.
Results may differ from the reference program's by a relative error of at most 0.00005.
Values sent between devices are 32-bit elements; how exact they have to be, the bound alone decides.
A program may use at most 64 MiB of HBM per device.

```python
import math
import jax
import jax.numpy as jnp
from jax import lax

Q = 4096
R = 32
POSITIONS = 8192


def truth(key):
    side = math.isqrt(Q)
    cell = jnp.arange(Q, dtype=jnp.int32)
    row_pos = (cell // side).astype(jnp.float32)
    col_pos = (cell % side).astype(jnp.float32)
    key_center = jax.random.fold_in(key, 101)
    key_radius = jax.random.fold_in(key, 102)
    key_amp = jax.random.fold_in(key, 103)
    key_gain = jax.random.fold_in(key, 104)
    key_block = jax.random.fold_in(key, 105)
    key_entry = jax.random.fold_in(key, 106)
    centers = jax.random.uniform(key_center, (R, 2), jnp.float32, 0.0, side - 1.0)
    radius = side * jax.random.uniform(key_radius, (R, 1), jnp.float32, 0.06, 0.2)
    amplitude = jax.random.uniform(key_amp, (R, 1), jnp.float32, 1.0, 2.0)
    gain = jax.random.uniform(key_gain, (Q,), jnp.float32, 0.5, 1.5)
    background = 0.15
    row_off = row_pos[None, :] - centers[:, 0:1]
    col_off = col_pos[None, :] - centers[:, 1:2]
    dist = row_off * row_off + col_off * col_off
    pattern = (background + amplitude * jnp.exp(-dist / (2.0 * radius * radius))) * gain[None, :]
    block_count = POSITIONS // 16
    block_scale = jnp.exp(jax.random.uniform(key_block, (R, block_count), jnp.float32, math.log(0.02), math.log(2.0)))
    entry = jax.random.uniform(key_entry, (R, POSITIONS), jnp.float32, 0.5, 1.5)
    abundance = jnp.repeat(block_scale, 16, axis=1) * entry
    return (pattern, abundance)


def draw_spectra(key, part):
    pattern, abundance = truth(key)
    clean = jnp.dot(abundance.T, pattern, precision=lax.Precision.HIGHEST)
    key_noise = jax.random.fold_in(key, 201)
    key_offset = jax.random.fold_in(key, 202)
    factor = jax.random.uniform(key_noise, (POSITIONS, Q), jnp.float32, 0.6, 1.4)
    offset = jax.random.uniform(key_offset, (POSITIONS, Q), jnp.float32, 0.0, 0.5)
    return clean * factor + offset


def draw_basis(key, part):
    pattern, abundance = truth(key)
    key_noise = jax.random.fold_in(key, 301)
    factor = jnp.exp(jax.random.uniform(key_noise, (R, Q), jnp.float32, math.log(0.5), math.log(2.0)))
    return pattern * factor


def draw_loadings(key, part):
    pattern, abundance = truth(key)
    key_noise = jax.random.fold_in(key, 401)
    factor = jnp.exp(jax.random.uniform(key_noise, (R, POSITIONS), jnp.float32, math.log(0.5), math.log(2.0)))
    return abundance * factor


def setup_inputs(seed: int = 0, part: int = 0) -> dict:
    splits = jax.random.split(jax.random.key(seed), 4)
    part_splits = jax.random.split(jax.random.fold_in(splits[3], part), 4)
    spectra = draw_spectra(jax.random.fold_in(jax.random.fold_in(splits[3], part), 71), part)
    basis = draw_basis(jax.random.fold_in(jax.random.fold_in(splits[3], part), 71), part)
    loadings = draw_loadings(jax.random.fold_in(jax.random.fold_in(splits[3], part), 71), part)
    return dict(spectra=spectra, basis=basis, loadings=loadings)


HIGHEST = lax.Precision.HIGHEST


def reference(spectra, basis, loadings):
    tied = 0.5 * (basis + jnp.flip(basis, 1))
    numer_h = lax.dot_general(tied, spectra, (((1,), (1,)), ((), ())), precision=HIGHEST)
    gram = lax.dot_general(tied, tied, (((1,), (1,)), ((), ())), precision=HIGHEST)
    new_loadings = loadings * numer_h / jnp.dot(gram, loadings, precision=HIGHEST)
    numer_w = jnp.dot(new_loadings, spectra, precision=HIGHEST)
    cross = lax.dot_general(new_loadings, new_loadings, (((1,), (1,)), ((), ())), precision=HIGHEST)
    tied_numer = 0.5 * (numer_w + jnp.flip(numer_w, 1))
    new_basis = tied * tied_numer / jnp.dot(cross, tied, precision=HIGHEST)
    return new_loadings, new_basis
```

```python
import functools

import jax
import jax.numpy as jnp
from jax import lax
from jax.experimental import pallas as pl
from jax.experimental.pallas import tpu as pltpu
from jax.sharding import PartitionSpec as P

HIGHEST = lax.Precision.HIGHEST
MESH = pl.DeviceIdType.MESH
F32 = jnp.float32
BF16 = jnp.bfloat16
LANES = 128


def split(x):
    hi = x.astype(BF16)
    lo = (x - hi.astype(F32)).astype(BF16)
    return hi, lo


def dot_nt(a, b):
    return lax.dot_general(a, b, (((1,), (1,)), ((), ())), preferred_element_type=F32)


def dot_nn(a, b):
    return lax.dot_general(a, b, (((1,), (0,)), ((), ())), preferred_element_type=F32)


def mirrored(x):
    index = (LANES - 1) - lax.broadcasted_iota(jnp.int32, x.shape, 1)
    return jnp.take_along_axis(x, index, axis=1, mode="promise_in_bounds")


def remote(src, dst, send, recv, where):
    return pltpu.make_async_remote_copy(
        src_ref=src, dst_ref=dst, send_sem=send, recv_sem=recv,
        device_id=where, device_id_type=MESH,
    )


def layout(n, rank, pixels):
    half = pixels // LANES // 2
    if n <= half:
        per, row_split = half // n, 1
    else:
        per, row_split = 1, min(n // half, rank // 8)
    return half, per, row_split


def piece_at(index, per, row_split, rows):
    first = index // row_split * per
    row = pl.multiple_of(lax.rem(index, row_split) * rows, 8) if row_split > 1 else 0
    return pl.ds(first, per), pl.ds(row, rows)


def divide(source, s_hi, s_lo, start, rows):
    @pl.loop(0, rows // 16, unroll=True)
    def _(j):
        part = pl.ds(pl.multiple_of(start + j * 16, 16), 16)
        hi, lo = split(source[part, :])
        s_hi[part, :] = hi
        s_lo[part, :] = lo


def tie_kernel(
    chunk, early,
    spectra, basis, loadings,
    s_hi, s_lo, tied3, tied2, load,
    sbuf, own, other, sp_sem, io_sem, bs_sem,
):
    rank, pixels = basis.shape
    blocks = pixels // LANES
    chunks = s_hi.shape[0] // chunk
    partner = {"det": 1 - lax.axis_index("det")}
    barrier = pltpu.get_barrier_semaphore()
    pl.semaphore_signal(barrier, inc=1, device_id=partner, device_id_type=MESH)

    spectra_copies = []
    for i in range(chunks):
        part = pl.ds(i * chunk, chunk)
        spectra_copies.append(
            pltpu.make_async_copy(spectra.at[part], sbuf.at[part], sp_sem.at[i])
        )
    own_copy = pltpu.make_async_copy(basis, own, io_sem.at[0])
    load_copy = pltpu.make_async_copy(loadings, load, io_sem.at[1])
    basis_copy = remote(basis, other, bs_sem.at[0], bs_sem.at[1], partner)
    for i in range(early):
        spectra_copies[i].start()
    pl.semaphore_wait(barrier, 1)
    basis_copy.start()
    own_copy.start()
    for i in range(early, chunks):
        spectra_copies[i].start()
    load_copy.start()

    for i in range(chunks - 1):
        spectra_copies[i].wait()
        divide(sbuf, s_hi, s_lo, i * chunk, chunk)
    own_copy.wait()
    basis_copy.wait()
    for b in range(blocks):
        mine = own[:, b * LANES:(b + 1) * LANES]
        back = blocks - 1 - b
        tied = 0.5 * (mine + mirrored(other[:, back * LANES:(back + 1) * LANES]))
        tied3[b] = tied
        hi, lo = split(tied)
        tied2[:rank, b * LANES:(b + 1) * LANES] = hi
        tied2[rank:, b * LANES:(b + 1) * LANES] = lo
    spectra_copies[chunks - 1].wait()
    divide(sbuf, s_hi, s_lo, (chunks - 1) * chunk, chunk)
    load_copy.wait()


def update_kernel(
    n, chunk, pos_chunk, col_chunk, wait_at,
    spectra, a_hi, a_lo, tied3, tied2, load,
    new_loadings, ag_in, fw_in,
    sbuf, b_hi, b_lo, weighted,
    nl2, num_out, num_in, w_keep, w_out, w_in, rs_in, cr_out, cr_in,
    sp_sem, nm_sem, w_sem, rs_send, rs_recv, cr_send, cr_recv,
    ag_send, ag_recv, fw_send, fw_recv,
):
    blocks, rank, _ = tied3.shape
    half, per, row_split = layout(n, rank, blocks * LANES)
    owners = half // per * row_split
    rows = rank // row_split
    pack = LANES // rank
    me = lax.axis_index("scan")
    partner = {"det": 1 - lax.axis_index("det")}
    first_rows = a_hi.shape[0]
    last_rows = b_hi.shape[0]

    def peer(k):
        return lax.rem(me + k, n)

    def source(k):
        return lax.rem(me + n - k, n)

    def owner_only(index, fn):
        if owners == n:
            fn()
        else:
            pl.when(index < owners)(fn)

    spectra_copies = []
    for i in range(last_rows // chunk):
        spectra_copies.append(
            pltpu.make_async_copy(
                spectra.at[pl.ds(first_rows + i * chunk, chunk)],
                sbuf.at[pl.ds(i * chunk, chunk)], sp_sem.at[i],
            )
        )
        spectra_copies[i].start()
    barrier = pltpu.get_barrier_semaphore()
    for k in range(1, n):
        pl.semaphore_signal(barrier, inc=1, device_id={"scan": peer(k)}, device_id_type=MESH)
    pl.semaphore_signal(barrier, inc=1, device_id=partner, device_id_type=MESH)
    positions = load.shape[1]
    chunks = positions // pos_chunk
    num_copies = [
        remote(num_out.at[i], num_in.at[i], nm_sem.at[0, i], nm_sem.at[1, i], partner)
        for i in range(chunks)
    ]

    def rows_of(start, size):
        if start < first_rows:
            return a_hi, a_lo, slice(start, start + size)
        return b_hi, b_lo, slice(start - first_rows, start - first_rows + size)

    def products(start):
        hi_ref, lo_ref, part = rows_of(start, chunk)
        both = dot_nt(hi_ref[part, :], tied2[...])
        low = dot_nt(lo_ref[part, :], tied2[:rank, :])
        at = start % pos_chunk
        num_out[start // pos_chunk, :, at:at + chunk] = (
            both[:, :rank] + (both[:, rank:] + low)
        ).T

    def send(i):
        if i == wait_at:
            pl.semaphore_wait(barrier, n)
            for j in range(i):
                num_copies[j].start()
        if i >= wait_at:
            num_copies[i].start()

    squares = dot_nt(tied2[...], tied2[...])
    gram = 2.0 * (
        squares[:rank, :rank] + (squares[:rank, rank:] + squares[rank:, :rank])
    )
    weighted[...] = jnp.dot(
        gram, load[...], precision=HIGHEST, preferred_element_type=F32
    )
    steps = positions // chunk
    for i in range(steps):
        later = (i + 1) * chunk - first_rows
        if 0 <= later < last_rows:
            spectra_copies[later // chunk].wait()
            divide(sbuf, b_hi, b_lo, later, chunk)
        products(i * chunk)
        if (i + 1) * chunk % pos_chunk == 0:
            send((i + 1) * chunk // pos_chunk - 1)

    def sums(i, cols):
        hi_ref, lo_ref, part = rows_of(i * pos_chunk, pos_chunk)
        where = slice(i * pos_chunk, (i + 1) * pos_chunk)
        both = dot_nn(nl2[:, where], hi_ref[part, cols])
        low = dot_nn(nl2[:rank, where], lo_ref[part, cols])
        return both[:rank] + (both[rank:] + low)

    step = col_chunk // LANES
    count = half // step

    def accumulate(i, target, first):
        for c in range(count):
            start = first + c * step
            value = sums(i, slice(start * LANES, (start + step) * LANES))
            for j in range(step):
                at = value[:, j * LANES:(j + 1) * LANES]
                if i == 0:
                    target[c * step + j] = at
                else:
                    target[c * step + j] = target[c * step + j] + at
            if target is w_out and i == chunks - 1:
                w_copies[c].start()

    w_copies = []
    for i in range(count):
        part = pl.ds(i * step, step)
        w_copies.append(
            remote(w_out.at[part], w_in.at[part], w_sem.at[0, i], w_sem.at[1, i], partner)
        )
    for i in range(chunks):
        num_copies[i].wait()
        cols = slice(i * pos_chunk, (i + 1) * pos_chunk)
        fresh = load[:, cols] * (num_out[i] + num_in[i]) / weighted[:, cols]
        new_loadings[:, cols] = fresh
        hi, lo = split(fresh)
        nl2[:rank, cols] = hi
        nl2[rank:, cols] = lo
        accumulate(i, w_out, half)
        if i < chunks - 1:
            accumulate(i, w_keep, 0)
    cr_copies = [None]
    for k in range(1, n):
        cr_copies.append(
            remote(cr_out, cr_in.at[k], cr_send.at[k], cr_recv.at[k], {"scan": peer(k)})
        )
    squares = dot_nt(nl2[...], nl2[...])
    cross = squares[:rank, :rank] + (squares[:rank, rank:] + squares[rank:, :rank])
    cr_out[...] = jnp.concatenate(
        [cross[i * (rank // pack):(i + 1) * (rank // pack)] for i in range(pack)], axis=1
    )
    for k in range(1, n):
        cr_copies[k].start()

    accumulate(chunks - 1, w_keep, 0)
    for copy in w_copies:
        copy.wait()
    for b in range(half):
        w_keep[b] = w_keep[b] + mirrored(w_in[half - 1 - b])

    rs_copies = [None]
    for k in range(1, n):
        rs_copies.append(
            remote(
                w_keep.at[piece_at(peer(k), per, row_split, rows)], rs_in.at[k],
                rs_send.at[k], rs_recv.at[k], {"scan": peer(k)},
            )
        )
        owner_only(peer(k), rs_copies[k].start)

    for k in range(1, n):
        cr_copies[k].wait_recv()
    total = cr_out[...]
    for k in range(1, n):
        total = total + cr_in[k]
    cross = jnp.concatenate(
        [total[:, i * rank:(i + 1) * rank] for i in range(pack)], axis=0
    )

    piece_buf = ag_in.at[0]
    ag_copies = [None]
    for k in range(1, n):
        ag_copies.append(
            remote(piece_buf, ag_in.at[k], ag_send.at[k], ag_recv.at[k], {"scan": peer(k)})
        )
    if owners == n:
        fw_copies = [remote(ag_in, fw_in, fw_send.at[0], fw_recv.at[0], partner)]
    else:
        fw_copies = [
            remote(ag_in.at[k], fw_in.at[k], fw_send.at[k], fw_recv.at[k], partner)
            for k in range(n)
        ]

    def own_piece():
        first, row = piece_at(me, per, row_split, rows)
        for j in range(per):
            weights = jnp.dot(
                cross, tied3[first.start + j], precision=HIGHEST, preferred_element_type=F32
            )
            if row_split > 1:
                piece_buf[0] = weights[:rows]
                for i in range(1, row_split):
                    @pl.when(lax.rem(me, row_split) == i)
                    def _():
                        piece_buf[0] = weights[i * rows:(i + 1) * rows]
            else:
                piece_buf[j] = weights
        for k in range(1, n):
            rs_copies[k].wait_recv()
        for j in range(per):
            total = w_keep[first.start + j, row, :]
            for k in range(1, n):
                total = total + rs_in[k, j]
            piece_buf[j] = tied3[first.start + j, row, :] * (0.5 * total) / piece_buf[j]
        for k in range(1, n):
            ag_copies[k].start()
        if owners < n:
            fw_copies[0].start()

    owner_only(me, own_piece)

    def arrived(k):
        def go():
            ag_copies[k].wait_recv()
            if owners < n:
                fw_copies[k].start()
        return go

    for k in range(1, n):
        owner_only(source(k), arrived(k))
    if owners == n:
        fw_copies[0].start()
    for k in range(1, n):
        cr_copies[k].wait_send()
        owner_only(peer(k), rs_copies[k].wait_send)
        owner_only(me, ag_copies[k].wait_send)
    for k, copy in enumerate(fw_copies):
        owner_only(source(k), copy.wait)


def output_kernel(
    n, fresh, ag_in, fw_in, new_loadings, new_basis, nb, io_sem
):
    rank, pixels = nb.shape
    half, per, row_split = layout(n, rank, pixels)
    owners = half // per * row_split
    rows = rank // row_split
    me = lax.axis_index("scan")
    first_copy = pltpu.make_async_copy(fresh, new_loadings, io_sem.at[0])
    first_copy.start()

    def put(index, ref, flip):
        first, row = piece_at(index, per, row_split, rows)
        for j in range(per):
            block = first.start + j
            value = ref[j]
            if flip:
                block = pixels // LANES - 1 - block
                value = mirrored(value)
            nb[row, pl.ds(pl.multiple_of(block * LANES, LANES), LANES)] = value

    for k in range(n):
        index = lax.rem(me + n - k, n)

        def go():
            put(index, ag_in.at[k], False)
            put(index, fw_in.at[k], True)

        if owners == n:
            go()
        else:
            pl.when(index < owners)(go)
    second_copy = pltpu.make_async_copy(nb, new_basis, io_sem.at[1])
    second_copy.start()
    first_copy.wait()
    second_copy.wait()


def per_device(n, spectra, basis, loadings):
    rank, pixels = basis.shape
    positions = loadings.shape[1]
    blocks = pixels // LANES
    half, per, row_split = layout(n, rank, pixels)
    rows = rank // row_split
    chunk = positions // 8
    first_rows = positions // 2
    last_rows = positions - first_rows
    pos_chunk = positions // 4
    col_chunk = 4 * LANES
    pack = LANES // rank
    dma = pltpu.SemaphoreType.DMA
    any_space = pl.BlockSpec(memory_space=pl.ANY)
    vmem = pl.BlockSpec(memory_space=pltpu.VMEM)
    hbm = pl.BlockSpec(memory_space=pltpu.HBM)
    inputs = [pltpu.with_memory_space_constraint(x, pltpu.HBM) for x in (spectra, basis, loadings)]
    parts = pl.pallas_call(
        functools.partial(tie_kernel, chunk, 2),
        out_shape=(
            pltpu.VMEM((first_rows, pixels), BF16),
            pltpu.VMEM((first_rows, pixels), BF16),
            pltpu.VMEM((blocks, rank, LANES), F32),
            pltpu.VMEM((2 * rank, pixels), BF16),
            pltpu.VMEM((rank, positions), F32),
        ),
        in_specs=[hbm] * 3,
        out_specs=(vmem,) * 5,
        scratch_shapes=[
            pltpu.VMEM((first_rows, pixels), F32),
            pltpu.VMEM((rank, pixels), F32),
            pltpu.VMEM((rank, pixels), F32),
            dma((first_rows // chunk,)),
            dma((2,)),
            dma((2,)),
        ],
        compiler_params=pltpu.CompilerParams(
            collective_id=0, has_side_effects=True, vmem_limit_bytes=32 << 20
        ),
        name="tie_and_split",
    )(*inputs)
    outs = pl.pallas_call(
        functools.partial(update_kernel, n, chunk, pos_chunk, col_chunk, 2),
        out_shape=(
            pltpu.VMEM(loadings.shape, F32),
            pltpu.VMEM((n, per, rows, LANES), F32),
            pltpu.VMEM((n, per, rows, LANES), F32),
        ),
        in_specs=[hbm] + [vmem] * 5,
        out_specs=(vmem,) * 3,
        scratch_shapes=[
            pltpu.VMEM((last_rows, pixels), F32),
            pltpu.VMEM((last_rows, pixels), BF16),
            pltpu.VMEM((last_rows, pixels), BF16),
            pltpu.VMEM((rank, positions), F32),
            pltpu.VMEM((2 * rank, positions), BF16),
            pltpu.VMEM((positions // pos_chunk, rank, pos_chunk), F32),
            pltpu.VMEM((positions // pos_chunk, rank, pos_chunk), F32),
            pltpu.VMEM((half, rank, LANES), F32),
            pltpu.VMEM((half, rank, LANES), F32),
            pltpu.VMEM((half, rank, LANES), F32),
            pltpu.VMEM((n, per, rows, LANES), F32),
            pltpu.VMEM((rank // pack, LANES), F32),
            pltpu.VMEM((n, rank // pack, LANES), F32),
            dma((last_rows // chunk,)),
            dma((2, positions // pos_chunk)),
            dma((2, half * LANES // col_chunk)),
            dma((n,)), dma((n,)), dma((n,)), dma((n,)),
            dma((n,)), dma((n,)), dma((n,)), dma((n,)),
        ],
        compiler_params=pltpu.CompilerParams(
            collective_id=1, has_side_effects=True, vmem_limit_bytes=40 << 20
        ),
        name="update",
    )(inputs[0], *parts)
    return pl.pallas_call(
        functools.partial(output_kernel, n),
        out_shape=(
            jax.ShapeDtypeStruct(loadings.shape, F32),
            jax.ShapeDtypeStruct(basis.shape, F32),
        ),
        in_specs=[vmem] * 3,
        out_specs=(any_space,) * 2,
        scratch_shapes=[pltpu.VMEM((rank, pixels), F32), dma((2,))],
        compiler_params=pltpu.CompilerParams(vmem_limit_bytes=8 << 20),
        name="write_out",
    )(*outs)


def solution(mesh):
    in_specs = (P(("grp", "scan"), "det"), P("grp", "det"), P("grp", "scan"))
    out_specs = (P("grp", "scan"), P("grp", "det"))
    return jax.shard_map(
        functools.partial(per_device, mesh.shape["scan"]),
        mesh=mesh, in_specs=in_specs, out_specs=out_specs, check_vma=False,
    )
```

```python
import functools

import jax
import jax.numpy as jnp
from jax import lax
from jax.experimental import pallas as pl
from jax.experimental.pallas import tpu as pltpu
from jax.sharding import PartitionSpec as P

HIGHEST = lax.Precision.HIGHEST
MESH = pl.DeviceIdType.MESH
F32 = jnp.float32
BF16 = jnp.bfloat16
LANES = 128


def split(x):
    hi = x.astype(BF16)
    lo = (x - hi.astype(F32)).astype(BF16)
    return hi, lo


def dot_nt(a, b):
    return lax.dot_general(a, b, (((1,), (1,)), ((), ())), preferred_element_type=F32)


def dot_nn(a, b):
    return lax.dot_general(a, b, (((1,), (0,)), ((), ())), preferred_element_type=F32)


def mirrored(x):
    index = (LANES - 1) - lax.broadcasted_iota(jnp.int32, x.shape, 1)
    return jnp.take_along_axis(x, index, axis=1, mode="promise_in_bounds")


def remote(src, dst, send, recv, where):
    return pltpu.make_async_remote_copy(
        src_ref=src, dst_ref=dst, send_sem=send, recv_sem=recv,
        device_id=where, device_id_type=MESH,
    )


def layout(n, rank, pixels):
    half = pixels // LANES // 2
    if n <= half:
        per, row_split = half // n, 1
    else:
        per, row_split = 1, min(n // half, rank // 8)
    return half, per, row_split


def piece_at(index, per, row_split, rows):
    first = index // row_split * per
    row = pl.multiple_of(lax.rem(index, row_split) * rows, 8) if row_split > 1 else 0
    return pl.ds(first, per), pl.ds(row, rows)


def divide(source, s_hi, s_lo, start, rows):
    @pl.loop(0, rows // 16, unroll=True)
    def _(j):
        part = pl.ds(pl.multiple_of(start + j * 16, 16), 16)
        hi, lo = split(source[part, :])
        s_hi[part, :] = hi
        s_lo[part, :] = lo


def update_kernel(
    n, chunk, early, pos_chunk, col_chunk,
    spectra, basis, loadings,
    new_loadings, ag_in, fw_in,
    sbuf, s_hi, s_lo, own, other, tied3, tied2, load, weighted,
    nl2, num_out, num_in, w_keep, w_out, w_in, rs_in, cr_out, cr_in,
    hello, ready, sp_sem, io_sem, bs_sem,
    nm_sem, w_sem, rs_send, rs_recv, cr_send, cr_recv,
    ag_send, ag_recv, fw_send, fw_recv,
):
    blocks, rank, _ = tied3.shape
    half, per, row_split = layout(n, rank, blocks * LANES)
    owners = half // per * row_split
    rows = rank // row_split
    pack = LANES // rank
    me = lax.axis_index("scan")
    det = lax.axis_index("det")
    partner = {"det": 1 - det}
    positions = load.shape[1]
    first_rows = positions // 2

    def peer(k):
        return lax.rem(me + k, n)

    def source(k):
        return lax.rem(me + n - k, n)

    def owner_only(index, fn):
        if owners == n:
            fn()
        else:
            pl.when(index < owners)(fn)

    barrier = pltpu.get_barrier_semaphore()

    @pl.when(det == 0)
    def _():
        pl.semaphore_signal(barrier, inc=1, device_id=partner, device_id_type=MESH)

    spectra_copies = []
    for i in range(positions // chunk):
        part = pl.ds(i * chunk, chunk)
        spectra_copies.append(
            pltpu.make_async_copy(spectra.at[part], sbuf.at[part], sp_sem.at[i])
        )
    own_copy = pltpu.make_async_copy(basis, own, io_sem.at[0])
    load_copy = pltpu.make_async_copy(loadings, load, io_sem.at[1])
    basis_copy = remote(basis, other, bs_sem.at[0], bs_sem.at[1], partner)
    for i in range(early):
        spectra_copies[i].start()

    @pl.when(det == 1)
    def _():
        pl.semaphore_wait(barrier, 1)
        pl.semaphore_signal(hello, inc=1, device_id=partner, device_id_type=MESH)
        basis_copy.start()

    @pl.when(det == 0)
    def _():
        pl.semaphore_wait(hello, 1)
        basis_copy.start()
        for k in range(1, n):
            pl.semaphore_signal(
                barrier, inc=1, device_id={"scan": peer(k)}, device_id_type=MESH
            )

    own_copy.start()
    for i in range(early, len(spectra_copies)):
        spectra_copies[i].start()
    load_copy.start()

    first_chunks = first_rows // chunk
    for i in range(first_chunks):
        spectra_copies[i].wait()
        divide(sbuf, s_hi, s_lo, i * chunk, chunk)
    own_copy.wait()
    basis_copy.wait_recv()
    for b in range(blocks):
        mine = own[:, b * LANES:(b + 1) * LANES]
        back = blocks - 1 - b
        tied = 0.5 * (mine + mirrored(other[:, back * LANES:(back + 1) * LANES]))
        tied3[b] = tied
        hi, lo = split(tied)
        tied2[:rank, b * LANES:(b + 1) * LANES] = hi
        tied2[rank:, b * LANES:(b + 1) * LANES] = lo
    load_copy.wait()

    chunks = positions // pos_chunk
    num_copies = [
        remote(num_out.at[i], num_in.at[i], nm_sem.at[0, i], nm_sem.at[1, i], partner)
        for i in range(chunks)
    ]

    def products(start):
        part = slice(start, start + chunk)
        both = dot_nt(s_hi[part, :], tied2[...])
        low = dot_nt(s_lo[part, :], tied2[:rank, :])
        at = start % pos_chunk
        num_out[start // pos_chunk, :, at:at + chunk] = (
            both[:, :rank] + (both[:, rank:] + low)
        ).T

    for i in range(first_chunks):
        products(i * chunk)
    squares = dot_nt(tied2[...], tied2[...])
    gram = 2.0 * (
        squares[:rank, :rank] + (squares[:rank, rank:] + squares[rank:, :rank])
    )
    weighted[...] = jnp.dot(
        gram, load[...], precision=HIGHEST, preferred_element_type=F32
    )
    for i in range(chunks // 2):
        num_copies[i].start()
    for copy in spectra_copies[first_chunks:]:
        copy.wait()
    divide(sbuf, s_hi, s_lo, first_rows, chunk)
    for i in range(first_chunks, positions // chunk):
        if (i + 1) * chunk < positions:
            divide(sbuf, s_hi, s_lo, (i + 1) * chunk, chunk)
        products(i * chunk)
    for i in range(chunks // 2, chunks):
        num_copies[i].start()

    def update(i):
        num_copies[i].wait_recv()
        cols = slice(i * pos_chunk, (i + 1) * pos_chunk)
        fresh = load[:, cols] * (num_out[i] + num_in[i]) / weighted[:, cols]
        new_loadings[:, cols] = fresh
        hi, lo = split(fresh)
        nl2[:rank, cols] = hi
        nl2[rank:, cols] = lo

    def sums(cols, where):
        both = dot_nn(nl2[:, where], s_hi[where, cols])
        low = dot_nn(nl2[:rank, where], s_lo[where, cols])
        return both[:rank] + (both[rank:] + low)

    step = col_chunk // LANES
    count = half // step

    def accumulate(target, first, i, where, add):
        start = first + i * step
        value = sums(slice(start * LANES, (start + step) * LANES), where)
        for j in range(step):
            at = value[:, j * LANES:(j + 1) * LANES]
            target[i * step + j] = target[i * step + j] + at if add else at

    w_copies = []
    for i in range(count):
        part = pl.ds(i * step, step)
        w_copies.append(
            remote(w_out.at[part], w_in.at[part], w_sem.at[0, i], w_sem.at[1, i], partner)
        )
    early_rows, late_rows = slice(0, first_rows), slice(first_rows, positions)
    for i in range(chunks // 2):
        update(i)
    for i in range(count):
        accumulate(w_out, half, i, early_rows, False)
    for i in range(count):
        accumulate(w_keep, 0, i, early_rows, False)

    @pl.when(det == 0)
    def _():
        pl.semaphore_wait(barrier, n - 1)
        pl.semaphore_signal(ready, inc=1, device_id=partner, device_id_type=MESH)

    for i in range(chunks // 2, chunks):
        update(i)
    for i in range(count):
        accumulate(w_out, half, i, late_rows, True)
        w_copies[i].start()

    @pl.when(det == 1)
    def _():
        pl.semaphore_wait(ready, 1)

    cr_copies = [None]
    for k in range(1, n):
        cr_copies.append(
            remote(cr_out, cr_in.at[k], cr_send.at[k], cr_recv.at[k], {"scan": peer(k)})
        )
    squares = dot_nt(nl2[...], nl2[...])
    cross = squares[:rank, :rank] + (squares[:rank, rank:] + squares[rank:, :rank])
    cr_out[...] = jnp.concatenate(
        [cross[i * (rank // pack):(i + 1) * (rank // pack)] for i in range(pack)], axis=1
    )
    for k in range(1, n):
        cr_copies[k].start()

    for i in range(count):
        accumulate(w_keep, 0, i, late_rows, True)

    rs_copies = [None]
    for k in range(1, n):
        rs_copies.append(
            remote(
                w_keep.at[piece_at(peer(k), per, row_split, rows)], rs_in.at[k],
                rs_send.at[k], rs_recv.at[k], {"scan": peer(k)},
            )
        )
    for i in range(count):
        w_copies[i].wait_recv()
        for j in range(step):
            b = half - 1 - (i * step + j)
            w_keep[b] = w_keep[b] + mirrored(w_in[half - 1 - b])
    for k in range(1, n):
        owner_only(peer(k), rs_copies[k].start)

    for k in range(1, n):
        cr_copies[k].wait_recv()
    total = cr_out[...]
    for k in range(1, n):
        total = total + cr_in[k]
    cross = jnp.concatenate(
        [total[:, i * rank:(i + 1) * rank] for i in range(pack)], axis=0
    )

    piece_buf = ag_in.at[0]
    ag_copies = [None]
    for k in range(1, n):
        ag_copies.append(
            remote(piece_buf, ag_in.at[k], ag_send.at[k], ag_recv.at[k], {"scan": peer(k)})
        )
    if owners == n:
        fw_copies = [remote(ag_in, fw_in, fw_send.at[0], fw_recv.at[0], partner)]
    else:
        fw_copies = [
            remote(ag_in.at[k], fw_in.at[k], fw_send.at[k], fw_recv.at[k], partner)
            for k in range(n)
        ]

    def own_piece():
        first, row = piece_at(me, per, row_split, rows)
        for j in range(per):
            weights = jnp.dot(
                cross, tied3[first.start + j], precision=HIGHEST, preferred_element_type=F32
            )
            if row_split > 1:
                piece_buf[0] = weights[:rows]
                for i in range(1, row_split):
                    @pl.when(lax.rem(me, row_split) == i)
                    def _():
                        piece_buf[0] = weights[i * rows:(i + 1) * rows]
            else:
                piece_buf[j] = weights
        for k in range(1, n):
            rs_copies[k].wait_recv()
        for j in range(per):
            total = w_keep[first.start + j, row, :]
            for k in range(1, n):
                total = total + rs_in[k, j]
            piece_buf[j] = tied3[first.start + j, row, :] * (0.5 * total) / piece_buf[j]
        for k in range(1, n):
            ag_copies[k].start()
        if owners < n:
            fw_copies[0].start()

    owner_only(me, own_piece)

    def arrived(k):
        def go():
            ag_copies[k].wait_recv()
            if owners < n:
                fw_copies[k].start()
        return go

    for k in range(1, n):
        owner_only(source(k), arrived(k))
    if owners == n:
        fw_copies[0].start()
    for k in range(1, n):
        cr_copies[k].wait_send()
        owner_only(peer(k), rs_copies[k].wait_send)
        owner_only(me, ag_copies[k].wait_send)
    for copy in [basis_copy] + num_copies + w_copies:
        copy.wait_send()
    for k, copy in enumerate(fw_copies):
        owner_only(source(k), copy.wait)


def output_kernel(
    n, fresh, ag_in, fw_in, new_loadings, new_basis, nb, io_sem
):
    rank, pixels = nb.shape
    half, per, row_split = layout(n, rank, pixels)
    owners = half // per * row_split
    rows = rank // row_split
    me = lax.axis_index("scan")
    first_copy = pltpu.make_async_copy(fresh, new_loadings, io_sem.at[0])
    first_copy.start()

    def put(index, ref, flip):
        first, row = piece_at(index, per, row_split, rows)
        for j in range(per):
            block = first.start + j
            value = ref[j]
            if flip:
                block = pixels // LANES - 1 - block
                value = mirrored(value)
            nb[row, pl.ds(pl.multiple_of(block * LANES, LANES), LANES)] = value

    for k in range(n):
        index = lax.rem(me + n - k, n)

        def go():
            put(index, ag_in.at[k], False)
            put(index, fw_in.at[k], True)

        if owners == n:
            go()
        else:
            pl.when(index < owners)(go)
    second_copy = pltpu.make_async_copy(nb, new_basis, io_sem.at[1])
    second_copy.start()
    first_copy.wait()
    second_copy.wait()


def per_device(n, spectra, basis, loadings):
    rank, pixels = basis.shape
    positions = loadings.shape[1]
    blocks = pixels // LANES
    half, per, row_split = layout(n, rank, pixels)
    rows = rank // row_split
    chunk = positions // 8
    pos_chunk = positions // 4
    col_chunk = 4 * LANES
    pack = LANES // rank
    dma = pltpu.SemaphoreType.DMA
    any_space = pl.BlockSpec(memory_space=pl.ANY)
    vmem = pl.BlockSpec(memory_space=pltpu.VMEM)
    hbm = pl.BlockSpec(memory_space=pltpu.HBM)
    inputs = [pltpu.with_memory_space_constraint(x, pltpu.HBM) for x in (spectra, basis, loadings)]
    outs = pl.pallas_call(
        functools.partial(update_kernel, n, chunk, 3, pos_chunk, col_chunk),
        out_shape=(
            pltpu.VMEM(loadings.shape, F32),
            pltpu.VMEM((n, per, rows, LANES), F32),
            pltpu.VMEM((n, per, rows, LANES), F32),
        ),
        in_specs=[hbm] * 3,
        out_specs=(vmem,) * 3,
        scratch_shapes=[
            pltpu.VMEM(spectra.shape, F32),
            pltpu.VMEM(spectra.shape, BF16),
            pltpu.VMEM(spectra.shape, BF16),
            pltpu.VMEM((rank, pixels), F32),
            pltpu.VMEM((rank, pixels), F32),
            pltpu.VMEM((blocks, rank, LANES), F32),
            pltpu.VMEM((2 * rank, pixels), BF16),
            pltpu.VMEM((rank, positions), F32),
            pltpu.VMEM((rank, positions), F32),
            pltpu.VMEM((2 * rank, positions), BF16),
            pltpu.VMEM((positions // pos_chunk, rank, pos_chunk), F32),
            pltpu.VMEM((positions // pos_chunk, rank, pos_chunk), F32),
            pltpu.VMEM((half, rank, LANES), F32),
            pltpu.VMEM((half, rank, LANES), F32),
            pltpu.VMEM((half, rank, LANES), F32),
            pltpu.VMEM((n, per, rows, LANES), F32),
            pltpu.VMEM((rank // pack, LANES), F32),
            pltpu.VMEM((n, rank // pack, LANES), F32),
            pltpu.SemaphoreType.REGULAR,
            pltpu.SemaphoreType.REGULAR,
            dma((positions // chunk,)),
            dma((2,)),
            dma((2,)),
            dma((2, positions // pos_chunk)),
            dma((2, half * LANES // col_chunk)),
            dma((n,)), dma((n,)), dma((n,)), dma((n,)),
            dma((n,)), dma((n,)), dma((n,)), dma((n,)),
        ],
        compiler_params=pltpu.CompilerParams(
            collective_id=0, has_side_effects=True, vmem_limit_bytes=40 << 20
        ),
        name="update",
    )(*inputs)
    return pl.pallas_call(
        functools.partial(output_kernel, n),
        out_shape=(
            jax.ShapeDtypeStruct(loadings.shape, F32),
            jax.ShapeDtypeStruct(basis.shape, F32),
        ),
        in_specs=[vmem] * 3,
        out_specs=(any_space,) * 2,
        scratch_shapes=[pltpu.VMEM((rank, pixels), F32), dma((2,))],
        compiler_params=pltpu.CompilerParams(vmem_limit_bytes=8 << 20),
        name="write_out",
    )(*outs)


def solution(mesh):
    in_specs = (P(("grp", "scan"), "det"), P("grp", "det"), P("grp", "scan"))
    out_specs = (P("grp", "scan"), P("grp", "det"))
    return jax.shard_map(
        functools.partial(per_device, mesh.shape["scan"]),
        mesh=mesh, in_specs=in_specs, out_specs=out_specs, check_vma=False,
    )
```

```python
import functools

import jax
import jax.numpy as jnp
from jax import lax
from jax.experimental import pallas as pl
from jax.experimental.pallas import tpu as pltpu
from jax.sharding import PartitionSpec as P

HIGHEST = lax.Precision.HIGHEST
MESH = pl.DeviceIdType.MESH
F32 = jnp.float32
BF16 = jnp.bfloat16
LANES = 128


def split(x):
    hi = x.astype(BF16)
    lo = (x - hi.astype(F32)).astype(BF16)
    return hi, lo


def dot_nt(a, b):
    return lax.dot_general(a, b, (((1,), (1,)), ((), ())), preferred_element_type=F32)


def dot_nn(a, b):
    return lax.dot_general(a, b, (((1,), (0,)), ((), ())), preferred_element_type=F32)


def product(a, b):
    a_hi, a_lo = split(a)
    b_hi, b_lo = split(b)
    return dot_nn(a_hi, b_hi) + (dot_nn(a_hi, b_lo) + dot_nn(a_lo, b_hi))


def mirrored(x):
    index = (LANES - 1) - lax.broadcasted_iota(jnp.int32, x.shape, 1)
    return jnp.take_along_axis(x, index, axis=1, mode="promise_in_bounds")


def remote(src, dst, send, recv, where):
    return pltpu.make_async_remote_copy(
        src_ref=src, dst_ref=dst, send_sem=send, recv_sem=recv,
        device_id=where, device_id_type=MESH,
    )


def layout(n, rank, pixels):
    half = pixels // LANES // 2
    if n <= half:
        per, row_split = half // n, 1
    else:
        per, row_split = 1, min(n // half, rank // 8)
    return half, per, row_split


def piece_at(index, per, row_split, rows):
    first = index // row_split * per
    row = pl.multiple_of(lax.rem(index, row_split) * rows, 8) if row_split > 1 else 0
    return pl.ds(first, per), pl.ds(row, rows)


def divide(source, s_hi, s_lo, start, rows):
    @pl.loop(0, rows // 16, unroll=True)
    def _(j):
        part = pl.ds(pl.multiple_of(start + j * 16, 16), 16)
        hi, lo = split(source[part, :])
        s_hi[part, :] = hi
        s_lo[part, :] = lo


def update_kernel(
    n, chunk, early, flight, pos_chunk, col_chunk,
    spectra, basis, loadings,
    new_loadings, ag_in, fw_in,
    sbuf, s_hi, s_lo, own, other, tied3, tied2, load, weighted,
    nl2, num_out, num_in, w_keep, w_out, w_in, rs_in, cr_out, cr_in,
    hello, ready, sp_sem, io_sem, bs_sem,
    nm_sem, w_sem, rs_send, rs_recv, cr_send, cr_recv,
    ag_send, ag_recv, fw_send, fw_recv,
):
    blocks, rank, _ = tied3.shape
    half, per, row_split = layout(n, rank, blocks * LANES)
    owners = half // per * row_split
    rows = rank // row_split
    pack = LANES // rank
    me = lax.axis_index("scan")
    det = lax.axis_index("det")
    partner = {"det": 1 - det}
    positions = load.shape[1]
    first_rows = positions // 2

    def peer(k):
        return lax.rem(me + k, n)

    def source(k):
        return lax.rem(me + n - k, n)

    def owner_only(index, fn):
        if owners == n:
            fn()
        else:
            pl.when(index < owners)(fn)

    barrier = pltpu.get_barrier_semaphore()

    @pl.when(det == 0)
    def _():
        pl.semaphore_signal(barrier, inc=1, device_id=partner, device_id_type=MESH)

    spectra_copies = []
    for i in range(positions // chunk):
        part = pl.ds(i * chunk, chunk)
        spectra_copies.append(
            pltpu.make_async_copy(spectra.at[part], sbuf.at[part], sp_sem.at[i])
        )
    own_copy = pltpu.make_async_copy(basis, own, io_sem.at[0])
    load_copy = pltpu.make_async_copy(loadings, load, io_sem.at[1])
    basis_copy = remote(basis, other, bs_sem.at[0], bs_sem.at[1], partner)
    for i in range(early):
        spectra_copies[i].start()

    @pl.when(det == 1)
    def _():
        pl.semaphore_wait(barrier, 1)
        pl.semaphore_signal(hello, inc=1, device_id=partner, device_id_type=MESH)
        basis_copy.start()

    @pl.when(det == 0)
    def _():
        pl.semaphore_wait(hello, 1)
        basis_copy.start()
        for k in range(1, n):
            pl.semaphore_signal(
                barrier, inc=1, device_id={"scan": peer(k)}, device_id_type=MESH
            )

    own_copy.start()
    load_copy.start()
    for i in range(early, flight):
        spectra_copies[i].start()

    first_chunks = first_rows // chunk
    for i in range(first_chunks):
        spectra_copies[i].wait()
        if i + flight < len(spectra_copies):
            spectra_copies[i + flight].start()
        divide(sbuf, s_hi, s_lo, i * chunk, chunk)
    own_copy.wait()
    basis_copy.wait_recv()
    for b in range(blocks):
        mine = own[:, b * LANES:(b + 1) * LANES]
        back = blocks - 1 - b
        tied = 0.5 * (mine + mirrored(other[:, back * LANES:(back + 1) * LANES]))
        tied3[b] = tied
        hi, lo = split(tied)
        tied2[:rank, b * LANES:(b + 1) * LANES] = hi
        tied2[rank:, b * LANES:(b + 1) * LANES] = lo
    load_copy.wait()

    chunks = positions // pos_chunk
    num_copies = [
        remote(num_out.at[i], num_in.at[i], nm_sem.at[0, i], nm_sem.at[1, i], partner)
        for i in range(chunks)
    ]

    def products(start):
        part = slice(start, start + chunk)
        both = dot_nt(s_hi[part, :], tied2[...])
        low = dot_nt(s_lo[part, :], tied2[:rank, :])
        at = start % pos_chunk
        num_out[start // pos_chunk, :, at:at + chunk] = (
            both[:, :rank] + (both[:, rank:] + low)
        ).T

    for i in range(first_chunks + flight, len(spectra_copies)):
        spectra_copies[i].start()
    for i in range(first_chunks):
        products(i * chunk)
    for i in range(chunks // 2):
        num_copies[i].start()
    for copy in spectra_copies[first_chunks:]:
        copy.wait()
    divide(sbuf, s_hi, s_lo, first_rows, chunk)
    for i in range(first_chunks, positions // chunk):
        if (i + 1) * chunk < positions:
            divide(sbuf, s_hi, s_lo, (i + 1) * chunk, chunk)
        products(i * chunk)
        if i == first_chunks:
            squares = dot_nt(tied2[...], tied2[...])
            gram = 2.0 * (
                squares[:rank, :rank] + (squares[:rank, rank:] + squares[rank:, :rank])
            )
            weighted[...] = product(gram, load[...])
    for i in range(chunks // 2, chunks):
        num_copies[i].start()

    def update(i):
        num_copies[i].wait_recv()
        cols = slice(i * pos_chunk, (i + 1) * pos_chunk)
        fresh = load[:, cols] * (num_out[i] + num_in[i]) / weighted[:, cols]
        new_loadings[:, cols] = fresh
        hi, lo = split(fresh)
        nl2[:rank, cols] = hi
        nl2[rank:, cols] = lo

    def sums(cols, where):
        both = dot_nn(nl2[:, where], s_hi[where, cols])
        low = dot_nn(nl2[:rank, where], s_lo[where, cols])
        return both[:rank] + (both[rank:] + low)

    step = col_chunk // LANES
    count = half // step

    def accumulate(target, first, i, where, add):
        start = first + i * step
        value = sums(slice(start * LANES, (start + step) * LANES), where)
        for j in range(step):
            at = value[:, j * LANES:(j + 1) * LANES]
            target[i * step + j] = target[i * step + j] + at if add else at

    w_copies = []
    for i in range(count):
        part = pl.ds(i * step, step)
        w_copies.append(
            remote(w_out.at[part], w_in.at[part], w_sem.at[0, i], w_sem.at[1, i], partner)
        )
    early_rows, late_rows = slice(0, first_rows), slice(first_rows, positions)
    for i in range(chunks // 2):
        update(i)
    for i in range(count):
        accumulate(w_out, half, i, early_rows, False)
    for i in range(count):
        accumulate(w_keep, 0, i, early_rows, False)

    @pl.when(det == 0)
    def _():
        pl.semaphore_wait(barrier, n - 1)
        pl.semaphore_signal(ready, inc=1, device_id=partner, device_id_type=MESH)

    for i in range(chunks // 2, chunks):
        update(i)
    for i in range(count):
        accumulate(w_out, half, i, late_rows, True)
        w_copies[i].start()

    @pl.when(det == 1)
    def _():
        pl.semaphore_wait(ready, 1)

    cr_copies = [None]
    for k in range(1, n):
        cr_copies.append(
            remote(cr_out, cr_in.at[k], cr_send.at[k], cr_recv.at[k], {"scan": peer(k)})
        )
    squares = dot_nt(nl2[...], nl2[...])
    cross = squares[:rank, :rank] + (squares[:rank, rank:] + squares[rank:, :rank])
    cr_out[...] = jnp.concatenate(
        [cross[i * (rank // pack):(i + 1) * (rank // pack)] for i in range(pack)], axis=1
    )
    for k in range(1, n):
        cr_copies[k].start()

    for i in range(count):
        accumulate(w_keep, 0, i, late_rows, True)

    rs_copies = [None]
    for k in range(1, n):
        rs_copies.append(
            remote(
                w_keep.at[piece_at(peer(k), per, row_split, rows)], rs_in.at[k],
                rs_send.at[k], rs_recv.at[k], {"scan": peer(k)},
            )
        )
    for i in range(count):
        w_copies[i].wait_recv()
        for j in range(step):
            b = half - 1 - (i * step + j)
            w_keep[b] = w_keep[b] + mirrored(w_in[half - 1 - b])
    for k in range(1, n):
        owner_only(peer(k), rs_copies[k].start)

    for k in range(1, n):
        cr_copies[k].wait_recv()
    total = cr_out[...]
    for k in range(1, n):
        total = total + cr_in[k]
    cross = jnp.concatenate(
        [total[:, i * rank:(i + 1) * rank] for i in range(pack)], axis=0
    )

    piece_buf = ag_in.at[0]
    ag_copies = [None]
    for k in range(1, n):
        ag_copies.append(
            remote(piece_buf, ag_in.at[k], ag_send.at[k], ag_recv.at[k], {"scan": peer(k)})
        )
    if owners == n:
        fw_copies = [remote(ag_in, fw_in, fw_send.at[0], fw_recv.at[0], partner)]
    else:
        fw_copies = [
            remote(ag_in.at[k], fw_in.at[k], fw_send.at[k], fw_recv.at[k], partner)
            for k in range(n)
        ]

    def own_piece():
        first, row = piece_at(me, per, row_split, rows)
        for j in range(per):
            weights = jnp.dot(
                cross, tied3[first.start + j], precision=HIGHEST, preferred_element_type=F32
            )
            if row_split > 1:
                piece_buf[0] = weights[:rows]
                for i in range(1, row_split):
                    @pl.when(lax.rem(me, row_split) == i)
                    def _():
                        piece_buf[0] = weights[i * rows:(i + 1) * rows]
            else:
                piece_buf[j] = weights
        for k in range(1, n):
            rs_copies[k].wait_recv()
        for j in range(per):
            total = w_keep[first.start + j, row, :]
            for k in range(1, n):
                total = total + rs_in[k, j]
            piece_buf[j] = tied3[first.start + j, row, :] * (0.5 * total) / piece_buf[j]
        for k in range(1, n):
            ag_copies[k].start()
        if owners < n:
            fw_copies[0].start()

    owner_only(me, own_piece)

    def arrived(k):
        def go():
            ag_copies[k].wait_recv()
            if owners < n:
                fw_copies[k].start()
        return go

    for k in range(1, n):
        owner_only(source(k), arrived(k))
    if owners == n:
        fw_copies[0].start()
    for k in range(1, n):
        cr_copies[k].wait_send()
        owner_only(peer(k), rs_copies[k].wait_send)
        owner_only(me, ag_copies[k].wait_send)
    for copy in [basis_copy] + num_copies + w_copies:
        copy.wait_send()
    for k, copy in enumerate(fw_copies):
        owner_only(source(k), copy.wait)


def output_kernel(
    n, fresh, ag_in, fw_in, new_loadings, new_basis, nb, io_sem
):
    rank, pixels = nb.shape
    half, per, row_split = layout(n, rank, pixels)
    owners = half // per * row_split
    rows = rank // row_split
    me = lax.axis_index("scan")
    first_copy = pltpu.make_async_copy(fresh, new_loadings, io_sem.at[0])
    first_copy.start()

    def put(index, ref, flip):
        first, row = piece_at(index, per, row_split, rows)
        for j in range(per):
            block = first.start + j
            value = ref[j]
            if flip:
                block = pixels // LANES - 1 - block
                value = mirrored(value)
            nb[row, pl.ds(pl.multiple_of(block * LANES, LANES), LANES)] = value

    for k in range(n):
        index = lax.rem(me + n - k, n)

        def go():
            put(index, ag_in.at[k], False)
            put(index, fw_in.at[k], True)

        if owners == n:
            go()
        else:
            pl.when(index < owners)(go)
    second_copy = pltpu.make_async_copy(nb, new_basis, io_sem.at[1])
    second_copy.start()
    first_copy.wait()
    second_copy.wait()


def per_device(n, spectra, basis, loadings):
    rank, pixels = basis.shape
    positions = loadings.shape[1]
    blocks = pixels // LANES
    half, per, row_split = layout(n, rank, pixels)
    rows = rank // row_split
    chunk = positions // 8
    pos_chunk = positions // 4
    col_chunk = 4 * LANES
    pack = LANES // rank
    dma = pltpu.SemaphoreType.DMA
    any_space = pl.BlockSpec(memory_space=pl.ANY)
    vmem = pl.BlockSpec(memory_space=pltpu.VMEM)
    hbm = pl.BlockSpec(memory_space=pltpu.HBM)
    inputs = [pltpu.with_memory_space_constraint(x, pltpu.HBM) for x in (spectra, basis, loadings)]
    outs = pl.pallas_call(
        functools.partial(update_kernel, n, chunk, 4, 4, pos_chunk, col_chunk),
        out_shape=(
            pltpu.VMEM(loadings.shape, F32),
            pltpu.VMEM((n, per, rows, LANES), F32),
            pltpu.VMEM((n, per, rows, LANES), F32),
        ),
        in_specs=[hbm] * 3,
        out_specs=(vmem,) * 3,
        scratch_shapes=[
            pltpu.VMEM(spectra.shape, F32),
            pltpu.VMEM(spectra.shape, BF16),
            pltpu.VMEM(spectra.shape, BF16),
            pltpu.VMEM((rank, pixels), F32),
            pltpu.VMEM((rank, pixels), F32),
            pltpu.VMEM((blocks, rank, LANES), F32),
            pltpu.VMEM((2 * rank, pixels), BF16),
            pltpu.VMEM((rank, positions), F32),
            pltpu.VMEM((rank, positions), F32),
            pltpu.VMEM((2 * rank, positions), BF16),
            pltpu.VMEM((positions // pos_chunk, rank, pos_chunk), F32),
            pltpu.VMEM((positions // pos_chunk, rank, pos_chunk), F32),
            pltpu.VMEM((half, rank, LANES), F32),
            pltpu.VMEM((half, rank, LANES), F32),
            pltpu.VMEM((half, rank, LANES), F32),
            pltpu.VMEM((n, per, rows, LANES), F32),
            pltpu.VMEM((rank // pack, LANES), F32),
            pltpu.VMEM((n, rank // pack, LANES), F32),
            pltpu.SemaphoreType.REGULAR,
            pltpu.SemaphoreType.REGULAR,
            dma((positions // chunk,)),
            dma((2,)),
            dma((2,)),
            dma((2, positions // pos_chunk)),
            dma((2, half * LANES // col_chunk)),
            dma((n,)), dma((n,)), dma((n,)), dma((n,)),
            dma((n,)), dma((n,)), dma((n,)), dma((n,)),
        ],
        compiler_params=pltpu.CompilerParams(
            collective_id=0, has_side_effects=True, vmem_limit_bytes=40 << 20
        ),
        name="update",
    )(*inputs)
    return pl.pallas_call(
        functools.partial(output_kernel, n),
        out_shape=(
            jax.ShapeDtypeStruct(loadings.shape, F32),
            jax.ShapeDtypeStruct(basis.shape, F32),
        ),
        in_specs=[vmem] * 3,
        out_specs=(any_space,) * 2,
        scratch_shapes=[pltpu.VMEM((rank, pixels), F32), dma((2,))],
        compiler_params=pltpu.CompilerParams(vmem_limit_bytes=8 << 20),
        name="write_out",
    )(*outs)


def solution(mesh):
    in_specs = (P(("grp", "scan"), "det"), P("grp", "det"), P("grp", "scan"))
    out_specs = (P("grp", "scan"), P("grp", "det"))
    return jax.shard_map(
        functools.partial(per_device, mesh.shape["scan"]),
        mesh=mesh, in_specs=in_specs, out_specs=out_specs, check_vma=False,
    )
```

```python
import functools

import jax
import jax.numpy as jnp
from jax import lax
from jax.experimental import pallas as pl
from jax.experimental.pallas import tpu as pltpu
from jax.sharding import PartitionSpec as P

HIGHEST = lax.Precision.HIGHEST
MESH = pl.DeviceIdType.MESH
F32 = jnp.float32
BF16 = jnp.bfloat16
LANES = 128


def split(x):
    hi = x.astype(BF16)
    lo = (x - hi.astype(F32)).astype(BF16)
    return hi, lo


def dot_nt(a, b):
    return lax.dot_general(a, b, (((1,), (1,)), ((), ())), preferred_element_type=F32)


def dot_nn(a, b):
    return lax.dot_general(a, b, (((1,), (0,)), ((), ())), preferred_element_type=F32)


def product(a, b):
    a_hi, a_lo = split(a)
    b_hi, b_lo = split(b)
    return dot_nn(a_hi, b_hi) + (dot_nn(a_hi, b_lo) + dot_nn(a_lo, b_hi))


def mirrored(x):
    index = (LANES - 1) - lax.broadcasted_iota(jnp.int32, x.shape, 1)
    return jnp.take_along_axis(x, index, axis=1, mode="promise_in_bounds")


def remote(src, dst, send, recv, where):
    return pltpu.make_async_remote_copy(
        src_ref=src, dst_ref=dst, send_sem=send, recv_sem=recv,
        device_id=where, device_id_type=MESH,
    )


def layout(n, rank, pixels):
    half = pixels // LANES // 2
    if n <= half:
        per, row_split = half // n, 1
    else:
        per, row_split = 1, min(n // half, rank // 8)
    return half, per, row_split


def piece_at(index, per, row_split, rows):
    first = index // row_split * per
    row = pl.multiple_of(lax.rem(index, row_split) * rows, 8) if row_split > 1 else 0
    return pl.ds(first, per), pl.ds(row, rows)


def divide(source, s_hi, s_lo, start, rows):
    @pl.loop(0, rows // 16, unroll=True)
    def _(j):
        part = pl.ds(pl.multiple_of(start + j * 16, 16), 16)
        hi, lo = split(source[part, :])
        s_hi[part, :] = hi
        s_lo[part, :] = lo


def update_kernel(
    n, chunk, early, flight, pos_chunk, col_chunk,
    spectra, basis, loadings,
    new_loadings, ag_in, fw_in,
    sbuf, s_hi, s_lo, own, other, tied3, tied2, load, weighted,
    nl2, num_out, num_in, w_keep, w_out, w_in, rs_in, cr_out, cr_in,
    hello, ready, sp_sem, io_sem, bs_sem,
    nm_sem, w_sem, rs_send, rs_recv, cr_send, cr_recv,
    ag_send, ag_recv, fw_send, fw_recv,
):
    blocks, rank, _ = tied3.shape
    half, per, row_split = layout(n, rank, blocks * LANES)
    owners = half // per * row_split
    rows = rank // row_split
    pack = LANES // rank
    me = lax.axis_index("scan")
    det = lax.axis_index("det")
    partner = {"det": 1 - det}
    positions = load.shape[1]
    first_rows = positions // 2
    first_chunks = first_rows // chunk
    single = owners == n

    def peer(k):
        return lax.rem(me + k, n)

    def source(k):
        return lax.rem(me + n - k, n)

    def slot(k):
        return 0 if single else k

    def group(buffer, send, recv):
        part = pl.ds(1, n - 1)
        return remote(buffer.at[part], buffer.at[part], send.at[0], recv.at[0], partner)

    def owner_only(index, fn):
        if owners == n:
            fn()
        else:
            pl.when(index < owners)(fn)

    barrier = pltpu.get_barrier_semaphore()

    @pl.when(det == 0)
    def _():
        pl.semaphore_signal(barrier, inc=1, device_id=partner, device_id_type=MESH)

    spectra_copies = []
    for i in range(positions // chunk):
        part = pl.ds(i * chunk, chunk)
        spectra_copies.append(
            pltpu.make_async_copy(
                spectra.at[part], sbuf.at[part], sp_sem.at[min(i, first_chunks)]
            )
        )
    late_part = pl.ds(first_rows, positions - first_rows)
    late_copy = pltpu.make_async_copy(
        spectra.at[late_part], sbuf.at[late_part], sp_sem.at[first_chunks]
    )
    own_copy = pltpu.make_async_copy(basis, own, io_sem.at[0])
    load_copy = pltpu.make_async_copy(loadings, load, io_sem.at[1])
    basis_copy = remote(basis, other, bs_sem.at[0], bs_sem.at[1], partner)
    for i in range(early):
        spectra_copies[i].start()

    @pl.when(det == 1)
    def _():
        pl.semaphore_wait(barrier, 1)
        pl.semaphore_signal(hello, inc=1, device_id=partner, device_id_type=MESH)
        basis_copy.start()

    @pl.when(det == 0)
    def _():
        pl.semaphore_wait(hello, 1)
        basis_copy.start()
        for k in range(1, n):
            pl.semaphore_signal(
                barrier, inc=1, device_id={"scan": peer(k)}, device_id_type=MESH
            )

    own_copy.start()
    load_copy.start()
    for i in range(early, flight):
        spectra_copies[i].start()

    for i in range(first_chunks):
        spectra_copies[i].wait()
        if i + flight < len(spectra_copies):
            spectra_copies[i + flight].start()
        divide(sbuf, s_hi, s_lo, i * chunk, chunk)
    own_copy.wait()
    basis_copy.wait_recv()
    for b in range(blocks):
        mine = own[:, b * LANES:(b + 1) * LANES]
        back = blocks - 1 - b
        tied = 0.5 * (mine + mirrored(other[:, back * LANES:(back + 1) * LANES]))
        tied3[b] = tied
        hi, lo = split(tied)
        tied2[:rank, b * LANES:(b + 1) * LANES] = hi
        tied2[rank:, b * LANES:(b + 1) * LANES] = lo
    load_copy.wait()

    chunks = positions // pos_chunk
    num_copies = []
    for i in range(2):
        part = pl.ds(i * (chunks // 2), chunks // 2)
        num_copies.append(
            remote(num_out.at[part], num_in.at[part], nm_sem.at[0, i], nm_sem.at[1, i], partner)
        )

    def products(start):
        part = slice(start, start + chunk)
        both = dot_nt(s_hi[part, :], tied2[...])
        low = dot_nt(s_lo[part, :], tied2[:rank, :])
        at = start % pos_chunk
        num_out[start // pos_chunk, :, at:at + chunk] = (
            both[:, :rank] + (both[:, rank:] + low)
        ).T

    for i in range(first_chunks + flight, len(spectra_copies)):
        spectra_copies[i].start()
    for i in range(first_chunks):
        products(i * chunk)
    num_copies[0].start()
    late_copy.wait()
    divide(sbuf, s_hi, s_lo, first_rows, chunk)
    for i in range(first_chunks, positions // chunk):
        if (i + 1) * chunk < positions:
            divide(sbuf, s_hi, s_lo, (i + 1) * chunk, chunk)
        products(i * chunk)
        if i == first_chunks:
            squares = dot_nt(tied2[...], tied2[...])
            gram = 2.0 * (
                squares[:rank, :rank] + (squares[:rank, rank:] + squares[rank:, :rank])
            )
            weighted[...] = product(gram, load[...])
    num_copies[1].start()

    def update(i):
        cols = slice(i * pos_chunk, (i + 1) * pos_chunk)
        fresh = load[:, cols] * (num_out[i] + num_in[i]) / weighted[:, cols]
        new_loadings[:, cols] = fresh
        hi, lo = split(fresh)
        nl2[:rank, cols] = hi
        nl2[rank:, cols] = lo

    def sums(cols, where):
        both = dot_nn(nl2[:, where], s_hi[where, cols])
        low = dot_nn(nl2[:rank, where], s_lo[where, cols])
        return both[:rank] + (both[rank:] + low)

    step = col_chunk // LANES
    count = half // step

    def accumulate(target, first, i, where, add):
        start = first + i * step
        value = sums(slice(start * LANES, (start + step) * LANES), where)
        for j in range(step):
            at = value[:, j * LANES:(j + 1) * LANES]
            target[i * step + j] = target[i * step + j] + at if add else at

    w_copies = []
    for i in range(count):
        part = pl.ds(i * step, step)
        w_copies.append(
            remote(w_out.at[part], w_in.at[part], w_sem.at[0, i], w_sem.at[1, i], partner)
        )
    early_rows, late_rows = slice(0, first_rows), slice(first_rows, positions)
    num_copies[0].wait_recv()
    for i in range(chunks // 2):
        update(i)
    for i in range(count):
        accumulate(w_out, half, i, early_rows, False)
    for i in range(count):
        accumulate(w_keep, 0, i, early_rows, False)

    @pl.when(det == 0)
    def _():
        pl.semaphore_wait(barrier, n - 1)
        pl.semaphore_signal(ready, inc=1, device_id=partner, device_id_type=MESH)

    num_copies[1].wait_recv()
    for i in range(chunks // 2, chunks):
        update(i)
    for i in range(count):
        accumulate(w_out, half, i, late_rows, True)
        w_copies[i].start()

    @pl.when(det == 1)
    def _():
        pl.semaphore_wait(ready, 1)

    cr_copies = [None]
    for k in range(1, n):
        cr_copies.append(
            remote(cr_out, cr_in.at[k], cr_send.at[0], cr_recv.at[0], {"scan": peer(k)})
        )
    squares = dot_nt(nl2[...], nl2[...])
    cross = squares[:rank, :rank] + (squares[:rank, rank:] + squares[rank:, :rank])
    cr_out[...] = jnp.concatenate(
        [cross[i * (rank // pack):(i + 1) * (rank // pack)] for i in range(pack)], axis=1
    )
    for k in range(1, n):
        cr_copies[k].start()

    for i in range(count):
        accumulate(w_keep, 0, i, late_rows, True)

    rs_copies = [None]
    for k in range(1, n):
        rs_copies.append(
            remote(
                w_keep.at[piece_at(peer(k), per, row_split, rows)], rs_in.at[k],
                rs_send.at[slot(k)], rs_recv.at[slot(k)], {"scan": peer(k)},
            )
        )
    for i in range(count):
        w_copies[i].wait_recv()
        for j in range(step):
            b = half - 1 - (i * step + j)
            w_keep[b] = w_keep[b] + mirrored(w_in[half - 1 - b])
    for k in range(1, n):
        owner_only(peer(k), rs_copies[k].start)

    group(cr_in, cr_send, cr_recv).wait_recv()
    total = cr_out[...]
    for k in range(1, n):
        total = total + cr_in[k]
    cross = jnp.concatenate(
        [total[:, i * rank:(i + 1) * rank] for i in range(pack)], axis=0
    )

    piece_buf = ag_in.at[0]
    ag_copies = [None]
    for k in range(1, n):
        ag_copies.append(
            remote(piece_buf, ag_in.at[k], ag_send.at[slot(k)], ag_recv.at[slot(k)], {"scan": peer(k)})
        )
    if single:
        fw_copies = [remote(ag_in, fw_in, fw_send.at[0], fw_recv.at[0], partner)]
    else:
        fw_copies = [
            remote(ag_in.at[k], fw_in.at[k], fw_send.at[k], fw_recv.at[k], partner)
            for k in range(n)
        ]

    def own_piece():
        first, row = piece_at(me, per, row_split, rows)
        for j in range(per):
            weights = jnp.dot(
                cross, tied3[first.start + j], precision=HIGHEST, preferred_element_type=F32
            )
            if row_split > 1:
                piece_buf[0] = weights[:rows]
                for i in range(1, row_split):
                    @pl.when(lax.rem(me, row_split) == i)
                    def _():
                        piece_buf[0] = weights[i * rows:(i + 1) * rows]
            else:
                piece_buf[j] = weights
        if single:
            group(rs_in, rs_send, rs_recv).wait_recv()
        else:
            for k in range(1, n):
                rs_copies[k].wait_recv()
        for j in range(per):
            total = w_keep[first.start + j, row, :]
            for k in range(1, n):
                total = total + rs_in[k, j]
            piece_buf[j] = tied3[first.start + j, row, :] * (0.5 * total) / piece_buf[j]
        for k in range(1, n):
            ag_copies[k].start()
        if not single:
            fw_copies[0].start()

    owner_only(me, own_piece)

    def arrived(k):
        def go():
            ag_copies[k].wait_recv()
            fw_copies[k].start()
        return go

    if single:
        group(ag_in, ag_send, ag_recv).wait_recv()
        fw_copies[0].start()
        group(rs_in, rs_send, rs_recv).wait_send()
        group(ag_in, ag_send, ag_recv).wait_send()
    else:
        for k in range(1, n):
            owner_only(source(k), arrived(k))
        for k in range(1, n):
            owner_only(peer(k), rs_copies[k].wait_send)
            owner_only(me, ag_copies[k].wait_send)
    group(cr_in, cr_send, cr_recv).wait_send()
    for copy in [basis_copy] + num_copies + w_copies:
        copy.wait_send()
    for k, copy in enumerate(fw_copies):
        owner_only(source(k), copy.wait)


def output_kernel(
    n, fresh, ag_in, fw_in, new_loadings, new_basis, nb, io_sem
):
    rank, pixels = nb.shape
    half, per, row_split = layout(n, rank, pixels)
    owners = half // per * row_split
    rows = rank // row_split
    me = lax.axis_index("scan")
    first_copy = pltpu.make_async_copy(fresh, new_loadings, io_sem.at[0])
    first_copy.start()

    def put(index, ref, flip):
        first, row = piece_at(index, per, row_split, rows)
        for j in range(per):
            block = first.start + j
            value = ref[j]
            if flip:
                block = pixels // LANES - 1 - block
                value = mirrored(value)
            nb[row, pl.ds(pl.multiple_of(block * LANES, LANES), LANES)] = value

    for k in range(n):
        index = lax.rem(me + n - k, n)

        def go():
            put(index, ag_in.at[k], False)
            put(index, fw_in.at[k], True)

        if owners == n:
            go()
        else:
            pl.when(index < owners)(go)
    second_copy = pltpu.make_async_copy(nb, new_basis, io_sem.at[1])
    second_copy.start()
    first_copy.wait()
    second_copy.wait()


def per_device(n, spectra, basis, loadings):
    rank, pixels = basis.shape
    positions = loadings.shape[1]
    blocks = pixels // LANES
    half, per, row_split = layout(n, rank, pixels)
    rows = rank // row_split
    slots = 1 if half // per * row_split == n else n
    chunk = positions // 8
    pos_chunk = positions // 4
    col_chunk = 4 * LANES
    pack = LANES // rank
    dma = pltpu.SemaphoreType.DMA
    any_space = pl.BlockSpec(memory_space=pl.ANY)
    vmem = pl.BlockSpec(memory_space=pltpu.VMEM)
    hbm = pl.BlockSpec(memory_space=pltpu.HBM)
    inputs = [pltpu.with_memory_space_constraint(x, pltpu.HBM) for x in (spectra, basis, loadings)]
    outs = pl.pallas_call(
        functools.partial(update_kernel, n, chunk, 4, 4, pos_chunk, col_chunk),
        out_shape=(
            pltpu.VMEM(loadings.shape, F32),
            pltpu.VMEM((n, per, rows, LANES), F32),
            pltpu.VMEM((n, per, rows, LANES), F32),
        ),
        in_specs=[hbm] * 3,
        out_specs=(vmem,) * 3,
        scratch_shapes=[
            pltpu.VMEM(spectra.shape, F32),
            pltpu.VMEM(spectra.shape, BF16),
            pltpu.VMEM(spectra.shape, BF16),
            pltpu.VMEM((rank, pixels), F32),
            pltpu.VMEM((rank, pixels), F32),
            pltpu.VMEM((blocks, rank, LANES), F32),
            pltpu.VMEM((2 * rank, pixels), BF16),
            pltpu.VMEM((rank, positions), F32),
            pltpu.VMEM((rank, positions), F32),
            pltpu.VMEM((2 * rank, positions), BF16),
            pltpu.VMEM((positions // pos_chunk, rank, pos_chunk), F32),
            pltpu.VMEM((positions // pos_chunk, rank, pos_chunk), F32),
            pltpu.VMEM((half, rank, LANES), F32),
            pltpu.VMEM((half, rank, LANES), F32),
            pltpu.VMEM((half, rank, LANES), F32),
            pltpu.VMEM((n, per, rows, LANES), F32),
            pltpu.VMEM((rank // pack, LANES), F32),
            pltpu.VMEM((n, rank // pack, LANES), F32),
            pltpu.SemaphoreType.REGULAR,
            pltpu.SemaphoreType.REGULAR,
            dma((positions // 2 // chunk + 1,)),
            dma((2,)),
            dma((2,)),
            dma((2, 2)),
            dma((2, half * LANES // col_chunk)),
            dma((slots,)), dma((slots,)), dma((1,)), dma((1,)),
            dma((slots,)), dma((slots,)), dma((slots,)), dma((slots,)),
        ],
        compiler_params=pltpu.CompilerParams(
            collective_id=0, has_side_effects=True, vmem_limit_bytes=40 << 20
        ),
        name="update",
    )(*inputs)
    return pl.pallas_call(
        functools.partial(output_kernel, n),
        out_shape=(
            jax.ShapeDtypeStruct(loadings.shape, F32),
            jax.ShapeDtypeStruct(basis.shape, F32),
        ),
        in_specs=[vmem] * 3,
        out_specs=(any_space,) * 2,
        scratch_shapes=[pltpu.VMEM((rank, pixels), F32), dma((2,))],
        compiler_params=pltpu.CompilerParams(vmem_limit_bytes=8 << 20),
        name="write_out",
    )(*outs)


def solution(mesh):
    in_specs = (P(("grp", "scan"), "det"), P("grp", "det"), P("grp", "scan"))
    out_specs = (P("grp", "scan"), P("grp", "det"))
    return jax.shard_map(
        functools.partial(per_device, mesh.shape["scan"]),
        mesh=mesh, in_specs=in_specs, out_specs=out_specs, check_vma=False,
    )
```

```python
import functools

import jax
import jax.numpy as jnp
from jax import lax
from jax.experimental import pallas as pl
from jax.experimental.pallas import tpu as pltpu
from jax.sharding import PartitionSpec as P

HIGHEST = lax.Precision.HIGHEST
MESH = pl.DeviceIdType.MESH
F32 = jnp.float32
BF16 = jnp.bfloat16
LANES = 128


def split(x):
    hi = x.astype(BF16)
    lo = (x - hi.astype(F32)).astype(BF16)
    return hi, lo


def dot_nt(a, b):
    return lax.dot_general(a, b, (((1,), (1,)), ((), ())), preferred_element_type=F32)


def dot_nn(a, b):
    return lax.dot_general(a, b, (((1,), (0,)), ((), ())), preferred_element_type=F32)


def product(a, b):
    a_hi, a_lo = split(a)
    b_hi, b_lo = split(b)
    return dot_nn(a_hi, b_hi) + (dot_nn(a_hi, b_lo) + dot_nn(a_lo, b_hi))


def mirrored(x):
    index = (LANES - 1) - lax.broadcasted_iota(jnp.int32, x.shape, 1)
    return jnp.take_along_axis(x, index, axis=1, mode="promise_in_bounds")


def remote(src, dst, send, recv, where):
    return pltpu.make_async_remote_copy(
        src_ref=src, dst_ref=dst, send_sem=send, recv_sem=recv,
        device_id=where, device_id_type=MESH,
    )


def layout(n, rank, pixels):
    half = pixels // LANES // 2
    if n <= half:
        per, row_split = half // n, 1
    else:
        per, row_split = 1, min(n // half, rank // 8)
    return half, per, row_split


def piece_at(index, per, row_split, rows):
    first = index // row_split * per
    row = pl.multiple_of(lax.rem(index, row_split) * rows, 8) if row_split > 1 else 0
    return pl.ds(first, per), pl.ds(row, rows)


def divide(source, s_hi, s_lo, start, rows):
    @pl.loop(0, rows // 16, unroll=True)
    def _(j):
        part = pl.ds(pl.multiple_of(start + j * 16, 16), 16)
        hi, lo = split(source[part, :])
        s_hi[part, :] = hi
        s_lo[part, :] = lo


def update_kernel(
    n, chunk, early, flight, pos_chunk, col_chunk,
    spectra, basis, loadings,
    new_loadings, ag_in, fw_in,
    sbuf, s_hi, s_lo, own, other, tied3, tied2, load, weighted,
    nl2, num_out, num_in, w_keep, w_out, w_in, rs_in, cr_out, cr_in,
    hello, ready, sp_sem, io_sem, bs_sem,
    nm_sem, w_sem, rs_send, rs_recv, cr_send, cr_recv,
    ag_send, ag_recv, fw_send, fw_recv,
):
    blocks, rank, _ = tied3.shape
    half, per, row_split = layout(n, rank, blocks * LANES)
    owners = half // per * row_split
    rows = rank // row_split
    pack = LANES // rank
    me = lax.axis_index("scan")
    det = lax.axis_index("det")
    partner = {"det": 1 - det}
    positions = load.shape[1]
    first_rows = positions // 2
    first_chunks = first_rows // chunk
    single = owners == n
    middle = max(n // 2, 1)

    def peer(k):
        return lax.rem(me + k, n)

    def source(k):
        return lax.rem(me + n - k, n)

    def slot(k):
        return 0 if single else k

    def group(buffer, send, recv):
        part = pl.ds(1, n - 1)
        return remote(buffer.at[part], buffer.at[part], send.at[0], recv.at[0], partner)

    def owner_only(index, fn):
        if owners == n:
            fn()
        else:
            pl.when(index < owners)(fn)

    barrier = pltpu.get_barrier_semaphore()

    @pl.when(det == 0)
    def _():
        pl.semaphore_signal(barrier, inc=1, device_id=partner, device_id_type=MESH)

    spectra_copies = []
    for i in range(positions // chunk):
        part = pl.ds(i * chunk, chunk)
        spectra_copies.append(
            pltpu.make_async_copy(
                spectra.at[part], sbuf.at[part], sp_sem.at[min(i, first_chunks)]
            )
        )
    late_part = pl.ds(first_rows, positions - first_rows)
    late_copy = pltpu.make_async_copy(
        spectra.at[late_part], sbuf.at[late_part], sp_sem.at[first_chunks]
    )
    own_copy = pltpu.make_async_copy(basis, own, io_sem.at[0])
    load_copy = pltpu.make_async_copy(loadings, load, io_sem.at[1])
    basis_copy = remote(basis, other, bs_sem.at[0], bs_sem.at[1], partner)
    for i in range(early):
        spectra_copies[i].start()

    @pl.when(det == 1)
    def _():
        pl.semaphore_wait(barrier, 1)
        pl.semaphore_signal(hello, inc=1, device_id=partner, device_id_type=MESH)
        basis_copy.start()

    @pl.when(det == 0)
    def _():
        pl.semaphore_wait(hello, 1)
        basis_copy.start()
        for k in range(1, n):
            pl.semaphore_signal(
                barrier, inc=1, device_id={"scan": peer(k)}, device_id_type=MESH
            )

    own_copy.start()
    load_copy.start()
    for i in range(early, flight):
        spectra_copies[i].start()

    for i in range(first_chunks):
        spectra_copies[i].wait()
        if i + flight < len(spectra_copies):
            spectra_copies[i + flight].start()
        divide(sbuf, s_hi, s_lo, i * chunk, chunk)
    own_copy.wait()
    basis_copy.wait_recv()
    for b in range(blocks):
        mine = own[:, b * LANES:(b + 1) * LANES]
        back = blocks - 1 - b
        tied = 0.5 * (mine + mirrored(other[:, back * LANES:(back + 1) * LANES]))
        tied3[b] = tied
        hi, lo = split(tied)
        tied2[:rank, b * LANES:(b + 1) * LANES] = hi
        tied2[rank:, b * LANES:(b + 1) * LANES] = lo
    load_copy.wait()

    chunks = positions // pos_chunk
    num_copies = []
    for i in range(2):
        part = pl.ds(i * (chunks // 2), chunks // 2)
        num_copies.append(
            remote(num_out.at[part], num_in.at[part], nm_sem.at[0, i], nm_sem.at[1, i], partner)
        )

    def products(start):
        part = slice(start, start + chunk)
        both = dot_nt(s_hi[part, :], tied2[...])
        low = dot_nt(s_lo[part, :], tied2[:rank, :])
        at = start % pos_chunk
        num_out[start // pos_chunk, :, at:at + chunk] = (
            both[:, :rank] + (both[:, rank:] + low)
        ).T

    for i in range(first_chunks + flight, len(spectra_copies)):
        spectra_copies[i].start()
    for i in range(first_chunks):
        products(i * chunk)
    num_copies[0].start()
    late_copy.wait()
    divide(sbuf, s_hi, s_lo, first_rows, chunk)
    for i in range(first_chunks, positions // chunk):
        if (i + 1) * chunk < positions:
            divide(sbuf, s_hi, s_lo, (i + 1) * chunk, chunk)
        products(i * chunk)
        if i == first_chunks:
            squares = dot_nt(tied2[...], tied2[...])
            gram = 2.0 * (
                squares[:rank, :rank] + (squares[:rank, rank:] + squares[rank:, :rank])
            )
            weighted[...] = product(gram, load[...])
    num_copies[1].start()

    def update(i):
        cols = slice(i * pos_chunk, (i + 1) * pos_chunk)
        fresh = load[:, cols] * (num_out[i] + num_in[i]) / weighted[:, cols]
        new_loadings[:, cols] = fresh
        hi, lo = split(fresh)
        nl2[:rank, cols] = hi
        nl2[rank:, cols] = lo

    def sums(cols, where):
        both = dot_nn(nl2[:, where], s_hi[where, cols])
        low = dot_nn(nl2[:rank, where], s_lo[where, cols])
        return both[:rank] + (both[rank:] + low)

    step = col_chunk // LANES
    count = half // step

    def accumulate(target, first, i, where, add):
        start = first + i * step
        value = sums(slice(start * LANES, (start + step) * LANES), where)
        for j in range(step):
            at = value[:, j * LANES:(j + 1) * LANES]
            target[i * step + j] = target[i * step + j] + at if add else at

    w_copies = []
    for i in range(count):
        part = pl.ds(i * step, step)
        w_copies.append(
            remote(w_out.at[part], w_in.at[part], w_sem.at[0, i], w_sem.at[1, i], partner)
        )
    early_rows, late_rows = slice(0, first_rows), slice(first_rows, positions)
    num_copies[0].wait_recv()
    for i in range(chunks // 2):
        update(i)
    for i in range(count):
        accumulate(w_out, half, i, early_rows, False)
    for i in range(count):
        accumulate(w_keep, 0, i, early_rows, False)

    @pl.when(det == 0)
    def _():
        pl.semaphore_wait(barrier, n - 1)
        pl.semaphore_signal(ready, inc=1, device_id=partner, device_id_type=MESH)

    num_copies[1].wait_recv()
    for i in range(chunks // 2, chunks):
        update(i)
    for i in range(count):
        accumulate(w_out, half, i, late_rows, True)
        w_copies[i].start()

    @pl.when(det == 1)
    def _():
        pl.semaphore_wait(ready, 1)

    cr_copies = [None]
    for k in range(1, n):
        cr_copies.append(
            remote(cr_out, cr_in.at[k], cr_send.at[0], cr_recv.at[0], {"scan": peer(k)})
        )
    squares = dot_nt(nl2[...], nl2[...])
    cross = squares[:rank, :rank] + (squares[:rank, rank:] + squares[rank:, :rank])
    cr_out[...] = jnp.concatenate(
        [cross[i * (rank // pack):(i + 1) * (rank // pack)] for i in range(pack)], axis=1
    )
    for k in range(1, n):
        cr_copies[k].start()

    for i in range(count):
        accumulate(w_keep, 0, i, late_rows, True)

    rs_copies = [None]
    for k in range(1, n):
        rs_copies.append(
            remote(
                w_keep.at[piece_at(peer(k), per, row_split, rows)], rs_in.at[k],
                rs_send.at[slot(k)], rs_recv.at[slot(k)], {"scan": peer(k)},
            )
        )
    for i in range(count):
        w_copies[i].wait_recv()
        for j in range(step):
            b = half - 1 - (i * step + j)
            w_keep[b] = w_keep[b] + mirrored(w_in[half - 1 - b])
    for k in range(1, n):
        owner_only(peer(k), rs_copies[k].start)

    group(cr_in, cr_send, cr_recv).wait_recv()
    total = cr_out[...]
    for k in range(1, n):
        total = total + cr_in[k]
    cross = jnp.concatenate(
        [total[:, i * rank:(i + 1) * rank] for i in range(pack)], axis=0
    )

    piece_buf = ag_in.at[0]
    ag_copies = [None]
    for k in range(1, n):
        ag_copies.append(
            remote(piece_buf, ag_in.at[k], ag_send.at[slot(k)], ag_recv.at[k // middle if single else k], {"scan": peer(k)})
        )
    if single:
        parts = [(low, min(low + middle, n)) for low in range(0, n, middle)]
        fw_copies = []
        for i, (low, high) in enumerate(parts):
            part = pl.ds(low, high - low)
            fw_copies.append(
                remote(ag_in.at[part], fw_in.at[part], fw_send.at[i], fw_recv.at[i], partner)
            )
    else:
        fw_copies = [
            remote(ag_in.at[k], fw_in.at[k], fw_send.at[k], fw_recv.at[k], partner)
            for k in range(n)
        ]

    def own_piece():
        first, row = piece_at(me, per, row_split, rows)
        for j in range(per):
            weights = jnp.dot(
                cross, tied3[first.start + j], precision=HIGHEST, preferred_element_type=F32
            )
            if row_split > 1:
                piece_buf[0] = weights[:rows]
                for i in range(1, row_split):
                    @pl.when(lax.rem(me, row_split) == i)
                    def _():
                        piece_buf[0] = weights[i * rows:(i + 1) * rows]
            else:
                piece_buf[j] = weights
        if single:
            group(rs_in, rs_send, rs_recv).wait_recv()
        else:
            for k in range(1, n):
                rs_copies[k].wait_recv()
        for j in range(per):
            total = w_keep[first.start + j, row, :]
            for k in range(1, n):
                total = total + rs_in[k, j]
            piece_buf[j] = tied3[first.start + j, row, :] * (0.5 * total) / piece_buf[j]
        for k in range(1, n):
            ag_copies[k].start()
        if not single:
            fw_copies[0].start()

    owner_only(me, own_piece)

    def arrived(k):
        def go():
            ag_copies[k].wait_recv()
            fw_copies[k].start()
        return go

    if single:
        for i, (low, high) in reversed(list(enumerate(parts))):
            part = pl.ds(max(low, 1), high - max(low, 1))
            if high > max(low, 1):
                remote(
                    ag_in.at[part], ag_in.at[part], ag_send.at[0], ag_recv.at[i], partner
                ).wait_recv()
            fw_copies[i].start()
        group(rs_in, rs_send, rs_recv).wait_send()
        group(ag_in, ag_send, ag_recv).wait_send()
    else:
        for k in range(1, n):
            owner_only(source(k), arrived(k))
        for k in range(1, n):
            owner_only(peer(k), rs_copies[k].wait_send)
            owner_only(me, ag_copies[k].wait_send)
    group(cr_in, cr_send, cr_recv).wait_send()
    for copy in [basis_copy] + num_copies + w_copies:
        copy.wait_send()
    for k, copy in enumerate(fw_copies):
        owner_only(source(k), copy.wait)


def output_kernel(
    n, fresh, ag_in, fw_in, new_loadings, new_basis, nb, io_sem
):
    rank, pixels = nb.shape
    half, per, row_split = layout(n, rank, pixels)
    owners = half // per * row_split
    rows = rank // row_split
    me = lax.axis_index("scan")
    first_copy = pltpu.make_async_copy(fresh, new_loadings, io_sem.at[0])
    first_copy.start()

    def put(index, ref, flip):
        first, row = piece_at(index, per, row_split, rows)
        for j in range(per):
            block = first.start + j
            value = ref[j]
            if flip:
                block = pixels // LANES - 1 - block
                value = mirrored(value)
            nb[row, pl.ds(pl.multiple_of(block * LANES, LANES), LANES)] = value

    copies = []
    for flip, ref in enumerate((ag_in, fw_in)):
        for k in range(n):
            index = lax.rem(me + n - k, n)

            def go():
                put(index, ref.at[k], flip)

            if owners == n:
                go()
            else:
                pl.when(index < owners)(go)
        part = pl.ds(flip * (pixels // 2), pixels // 2)
        copies.append(
            pltpu.make_async_copy(nb.at[:, part], new_basis.at[:, part], io_sem.at[1 + flip])
        )
        copies[flip].start()
    first_copy.wait()
    for copy in copies:
        copy.wait()


def per_device(n, spectra, basis, loadings):
    rank, pixels = basis.shape
    positions = loadings.shape[1]
    blocks = pixels // LANES
    half, per, row_split = layout(n, rank, pixels)
    rows = rank // row_split
    slots = 1 if half // per * row_split == n else n
    chunk = positions // 8
    pos_chunk = positions // 4
    col_chunk = 4 * LANES
    pack = LANES // rank
    dma = pltpu.SemaphoreType.DMA
    any_space = pl.BlockSpec(memory_space=pl.ANY)
    vmem = pl.BlockSpec(memory_space=pltpu.VMEM)
    hbm = pl.BlockSpec(memory_space=pltpu.HBM)
    inputs = [pltpu.with_memory_space_constraint(x, pltpu.HBM) for x in (spectra, basis, loadings)]
    outs = pl.pallas_call(
        functools.partial(update_kernel, n, chunk, 4, 4, pos_chunk, col_chunk),
        out_shape=(
            pltpu.VMEM(loadings.shape, F32),
            pltpu.VMEM((n, per, rows, LANES), F32),
            pltpu.VMEM((n, per, rows, LANES), F32),
        ),
        in_specs=[hbm] * 3,
        out_specs=(vmem,) * 3,
        scratch_shapes=[
            pltpu.VMEM(spectra.shape, F32),
            pltpu.VMEM(spectra.shape, BF16),
            pltpu.VMEM(spectra.shape, BF16),
            pltpu.VMEM((rank, pixels), F32),
            pltpu.VMEM((rank, pixels), F32),
            pltpu.VMEM((blocks, rank, LANES), F32),
            pltpu.VMEM((2 * rank, pixels), BF16),
            pltpu.VMEM((rank, positions), F32),
            pltpu.VMEM((rank, positions), F32),
            pltpu.VMEM((2 * rank, positions), BF16),
            pltpu.VMEM((positions // pos_chunk, rank, pos_chunk), F32),
            pltpu.VMEM((positions // pos_chunk, rank, pos_chunk), F32),
            pltpu.VMEM((half, rank, LANES), F32),
            pltpu.VMEM((half, rank, LANES), F32),
            pltpu.VMEM((half, rank, LANES), F32),
            pltpu.VMEM((n, per, rows, LANES), F32),
            pltpu.VMEM((rank // pack, LANES), F32),
            pltpu.VMEM((n, rank // pack, LANES), F32),
            pltpu.SemaphoreType.REGULAR,
            pltpu.SemaphoreType.REGULAR,
            dma((positions // 2 // chunk + 1,)),
            dma((2,)),
            dma((2,)),
            dma((2, 2)),
            dma((2, half * LANES // col_chunk)),
            dma((slots,)), dma((slots,)), dma((1,)), dma((1,)),
            dma((slots,)), dma((max(slots, 2),)), dma((max(slots, 2),)), dma((max(slots, 2),)),
        ],
        compiler_params=pltpu.CompilerParams(
            collective_id=0, has_side_effects=True, vmem_limit_bytes=40 << 20
        ),
        name="update",
    )(*inputs)
    return pl.pallas_call(
        functools.partial(output_kernel, n),
        out_shape=(
            jax.ShapeDtypeStruct(loadings.shape, F32),
            jax.ShapeDtypeStruct(basis.shape, F32),
        ),
        in_specs=[vmem] * 3,
        out_specs=(any_space,) * 2,
        scratch_shapes=[pltpu.VMEM((rank, pixels), F32), dma((3,))],
        compiler_params=pltpu.CompilerParams(vmem_limit_bytes=8 << 20),
        name="write_out",
    )(*outs)


def solution(mesh):
    in_specs = (P(("grp", "scan"), "det"), P("grp", "det"), P("grp", "scan"))
    out_specs = (P("grp", "scan"), P("grp", "det"))
    return jax.shard_map(
        functools.partial(per_device, mesh.shape["scan"]),
        mesh=mesh, in_specs=in_specs, out_specs=out_specs, check_vma=False,
    )
```

```python
import functools

import jax
import jax.numpy as jnp
from jax import lax
from jax.experimental import pallas as pl
from jax.experimental.pallas import tpu as pltpu
from jax.sharding import PartitionSpec as P

HIGHEST = lax.Precision.HIGHEST
MESH = pl.DeviceIdType.MESH
F32 = jnp.float32
BF16 = jnp.bfloat16
LANES = 128


def split(x):
    hi = x.astype(BF16)
    lo = (x - hi.astype(F32)).astype(BF16)
    return hi, lo


def dot_nt(a, b):
    return lax.dot_general(a, b, (((1,), (1,)), ((), ())), preferred_element_type=F32)


def dot_nn(a, b):
    return lax.dot_general(a, b, (((1,), (0,)), ((), ())), preferred_element_type=F32)


def product(a, b):
    a_hi, a_lo = split(a)
    b_hi, b_lo = split(b)
    return dot_nn(a_hi, b_hi) + (dot_nn(a_hi, b_lo) + dot_nn(a_lo, b_hi))


def mirrored(x):
    index = (LANES - 1) - lax.broadcasted_iota(jnp.int32, x.shape, 1)
    return jnp.take_along_axis(x, index, axis=1, mode="promise_in_bounds")


def remote(src, dst, send, recv, where):
    return pltpu.make_async_remote_copy(
        src_ref=src, dst_ref=dst, send_sem=send, recv_sem=recv,
        device_id=where, device_id_type=MESH,
    )


def layout(n, rank, pixels):
    half = pixels // LANES // 2
    if n <= half:
        per, row_split = half // n, 1
    else:
        per, row_split = 1, min(n // half, rank // 8)
    return half, per, row_split


def piece_at(index, per, row_split, rows):
    first = index // row_split * per
    row = pl.multiple_of(lax.rem(index, row_split) * rows, 8) if row_split > 1 else 0
    return pl.ds(first, per), pl.ds(row, rows)


def divide(source, s_hi, s_lo, start, rows):
    @pl.loop(0, rows // 16, unroll=True)
    def _(j):
        part = pl.ds(pl.multiple_of(start + j * 16, 16), 16)
        hi, lo = split(source[part, :])
        s_hi[part, :] = hi
        s_lo[part, :] = lo


def update_kernel(
    n, chunk, early, flight, pos_chunk, col_chunk,
    spectra, basis, loadings,
    new_loadings, ag_in, fw_in,
    sbuf, s_hi, s_lo, own, other, tied3, tied2, load, weighted,
    nl2, num_out, num_in, w_keep, w_out, w_in, rs_in, cr_out, cr_in,
    hello, ready, sp_sem, io_sem, bs_sem,
    nm_sem, w_sem, rs_send, rs_recv, cr_send, cr_recv,
    ag_send, ag_recv, fw_send, fw_recv,
):
    blocks, rank, _ = tied3.shape
    half, per, row_split = layout(n, rank, blocks * LANES)
    owners = half // per * row_split
    rows = rank // row_split
    pack = LANES // rank
    me = lax.axis_index("scan")
    det = lax.axis_index("det")
    partner = {"det": 1 - det}
    positions = load.shape[1]
    first_rows = positions // 2
    first_chunks = first_rows // chunk
    single = owners == n
    middle = max(n // 2, 1)

    def peer(k):
        return lax.rem(me + k, n)

    def source(k):
        return lax.rem(me + n - k, n)

    def slot(k):
        return 0 if single else k

    def group(buffer, send, recv):
        part = pl.ds(1, n - 1)
        return remote(buffer.at[part], buffer.at[part], send.at[0], recv.at[0], partner)

    def owner_only(index, fn):
        if owners == n:
            fn()
        else:
            pl.when(index < owners)(fn)

    barrier = pltpu.get_barrier_semaphore()

    @pl.when(det == 0)
    def _():
        pl.semaphore_signal(barrier, inc=1, device_id=partner, device_id_type=MESH)

    spectra_copies = []
    for i in range(positions // chunk):
        part = pl.ds(i * chunk, chunk)
        spectra_copies.append(
            pltpu.make_async_copy(
                spectra.at[part], sbuf.at[part], sp_sem.at[min(i, first_chunks)]
            )
        )
    late_part = pl.ds(first_rows, positions - first_rows)
    late_copy = pltpu.make_async_copy(
        spectra.at[late_part], sbuf.at[late_part], sp_sem.at[first_chunks]
    )
    own_copy = pltpu.make_async_copy(basis, own, io_sem.at[0])
    load_copy = pltpu.make_async_copy(loadings, load, io_sem.at[1])
    basis_copy = remote(basis, other, bs_sem.at[0], bs_sem.at[1], partner)
    for i in range(early):
        spectra_copies[i].start()

    @pl.when(det == 1)
    def _():
        pl.semaphore_wait(barrier, 1)
        pl.semaphore_signal(hello, inc=1, device_id=partner, device_id_type=MESH)
        basis_copy.start()

    @pl.when(det == 0)
    def _():
        pl.semaphore_wait(hello, 1)
        basis_copy.start()
        for k in range(1, n):
            pl.semaphore_signal(
                barrier, inc=1, device_id={"scan": peer(k)}, device_id_type=MESH
            )

    own_copy.start()
    load_copy.start()
    for i in range(early, flight):
        spectra_copies[i].start()

    for i in range(first_chunks):
        spectra_copies[i].wait()
        if i + flight < len(spectra_copies):
            spectra_copies[i + flight].start()
        divide(sbuf, s_hi, s_lo, i * chunk, chunk)
    own_copy.wait()
    basis_copy.wait_recv()
    for b in range(blocks):
        mine = own[:, b * LANES:(b + 1) * LANES]
        back = blocks - 1 - b
        tied = 0.5 * (mine + mirrored(other[:, back * LANES:(back + 1) * LANES]))
        tied3[b] = tied
        hi, lo = split(tied)
        tied2[:rank, b * LANES:(b + 1) * LANES] = hi
        tied2[rank:, b * LANES:(b + 1) * LANES] = lo
    load_copy.wait()

    chunks = positions // pos_chunk
    num_copies = []
    for i in range(2):
        part = pl.ds(i * (chunks // 2), chunks // 2)
        num_copies.append(
            remote(num_out.at[part], num_in.at[part], nm_sem.at[0, i], nm_sem.at[1, i], partner)
        )

    def products(start, size=chunk):
        part = slice(start, start + size)
        both = dot_nt(s_hi[part, :], tied2[...])
        low = dot_nt(s_lo[part, :], tied2[:rank, :])
        at = start % pos_chunk
        num_out[start // pos_chunk, :, at:at + size] = (
            both[:, :rank] + (both[:, rank:] + low)
        ).T

    for i in range(first_chunks + flight, len(spectra_copies)):
        spectra_copies[i].start()
    for start in range(0, first_rows, pos_chunk):
        products(start, pos_chunk)
    num_copies[0].start()
    late_copy.wait()
    divide(sbuf, s_hi, s_lo, first_rows, chunk)
    for i in range(first_chunks, positions // chunk):
        if (i + 1) * chunk < positions:
            divide(sbuf, s_hi, s_lo, (i + 1) * chunk, chunk)
        products(i * chunk)
        if i == first_chunks:
            squares = dot_nt(tied2[...], tied2[...])
            gram = 2.0 * (
                squares[:rank, :rank] + (squares[:rank, rank:] + squares[rank:, :rank])
            )
            weighted[...] = product(gram, load[...])
    num_copies[1].start()

    def update(i):
        cols = slice(i * pos_chunk, (i + 1) * pos_chunk)
        fresh = load[:, cols] * (num_out[i] + num_in[i]) / weighted[:, cols]
        new_loadings[:, cols] = fresh
        hi, lo = split(fresh)
        nl2[:rank, cols] = hi
        nl2[rank:, cols] = lo

    def sums(cols, where):
        both = dot_nn(nl2[:, where], s_hi[where, cols])
        low = dot_nn(nl2[:rank, where], s_lo[where, cols])
        return both[:rank] + (both[rank:] + low)

    step = col_chunk // LANES
    count = half // step

    def accumulate(target, first, i, where, add):
        start = first + i * step
        value = sums(slice(start * LANES, (start + step) * LANES), where)
        for j in range(step):
            at = value[:, j * LANES:(j + 1) * LANES]
            target[i * step + j] = target[i * step + j] + at if add else at

    w_copies = []
    for i in range(count):
        part = pl.ds(i * step, step)
        w_copies.append(
            remote(w_out.at[part], w_in.at[part], w_sem.at[0, i], w_sem.at[1, i], partner)
        )
    early_rows, late_rows = slice(0, first_rows), slice(first_rows, positions)
    num_copies[0].wait_recv()
    for i in range(chunks // 2):
        update(i)
    for i in range(count):
        accumulate(w_out, half, i, early_rows, False)
    for i in range(count):
        accumulate(w_keep, 0, i, early_rows, False)

    @pl.when(det == 0)
    def _():
        pl.semaphore_wait(barrier, n - 1)
        pl.semaphore_signal(ready, inc=1, device_id=partner, device_id_type=MESH)

    num_copies[1].wait_recv()
    for i in range(chunks // 2, chunks):
        update(i)
    for i in range(count):
        accumulate(w_out, half, i, late_rows, True)
        w_copies[i].start()

    @pl.when(det == 1)
    def _():
        pl.semaphore_wait(ready, 1)

    cr_copies = [None]
    for k in range(1, n):
        cr_copies.append(
            remote(cr_out, cr_in.at[k], cr_send.at[0], cr_recv.at[0], {"scan": peer(k)})
        )
    squares = dot_nt(nl2[...], nl2[...])
    cross = squares[:rank, :rank] + (squares[:rank, rank:] + squares[rank:, :rank])
    cr_out[...] = jnp.concatenate(
        [cross[i * (rank // pack):(i + 1) * (rank // pack)] for i in range(pack)], axis=1
    )
    for k in range(1, n):
        cr_copies[k].start()

    for i in range(count):
        accumulate(w_keep, 0, i, late_rows, True)

    rs_copies = [None]
    for k in range(1, n):
        rs_copies.append(
            remote(
                w_keep.at[piece_at(peer(k), per, row_split, rows)], rs_in.at[k],
                rs_send.at[slot(k)], rs_recv.at[slot(k)], {"scan": peer(k)},
            )
        )
    for i in range(count):
        w_copies[i].wait_recv()
        for j in range(step):
            b = half - 1 - (i * step + j)
            w_keep[b] = w_keep[b] + mirrored(w_in[half - 1 - b])
    for k in range(1, n):
        owner_only(peer(k), rs_copies[k].start)

    group(cr_in, cr_send, cr_recv).wait_recv()
    total = cr_out[...]
    for k in range(1, n):
        total = total + cr_in[k]
    cross = jnp.concatenate(
        [total[:, i * rank:(i + 1) * rank] for i in range(pack)], axis=0
    )

    piece_buf = ag_in.at[0]
    ag_copies = [None]
    for k in range(1, n):
        ag_copies.append(
            remote(piece_buf, ag_in.at[k], ag_send.at[slot(k)], ag_recv.at[k // middle if single else k], {"scan": peer(k)})
        )
    if single:
        parts = [(low, min(low + middle, n)) for low in range(0, n, middle)]
        fw_copies = []
        for i, (low, high) in enumerate(parts):
            part = pl.ds(low, high - low)
            fw_copies.append(
                remote(ag_in.at[part], fw_in.at[part], fw_send.at[i], fw_recv.at[i], partner)
            )
    else:
        fw_copies = [
            remote(ag_in.at[k], fw_in.at[k], fw_send.at[k], fw_recv.at[k], partner)
            for k in range(n)
        ]

    def own_piece():
        first, row = piece_at(me, per, row_split, rows)
        for j in range(per):
            weights = jnp.dot(
                cross, tied3[first.start + j], precision=HIGHEST, preferred_element_type=F32
            )
            if row_split > 1:
                piece_buf[0] = weights[:rows]
                for i in range(1, row_split):
                    @pl.when(lax.rem(me, row_split) == i)
                    def _():
                        piece_buf[0] = weights[i * rows:(i + 1) * rows]
            else:
                piece_buf[j] = weights
        if single:
            group(rs_in, rs_send, rs_recv).wait_recv()
        else:
            for k in range(1, n):
                rs_copies[k].wait_recv()
        for j in range(per):
            total = w_keep[first.start + j, row, :]
            for k in range(1, n):
                total = total + rs_in[k, j]
            piece_buf[j] = tied3[first.start + j, row, :] * (0.5 * total) / piece_buf[j]
        for k in range(1, n):
            ag_copies[k].start()
        if not single:
            fw_copies[0].start()

    owner_only(me, own_piece)

    def arrived(k):
        def go():
            ag_copies[k].wait_recv()
            fw_copies[k].start()
        return go

    if single:
        for i, (low, high) in reversed(list(enumerate(parts))):
            part = pl.ds(max(low, 1), high - max(low, 1))
            if high > max(low, 1):
                remote(
                    ag_in.at[part], ag_in.at[part], ag_send.at[0], ag_recv.at[i], partner
                ).wait_recv()
            fw_copies[i].start()
        group(rs_in, rs_send, rs_recv).wait_send()
        group(ag_in, ag_send, ag_recv).wait_send()
    else:
        for k in range(1, n):
            owner_only(source(k), arrived(k))
        for k in range(1, n):
            owner_only(peer(k), rs_copies[k].wait_send)
            owner_only(me, ag_copies[k].wait_send)
    group(cr_in, cr_send, cr_recv).wait_send()
    for copy in [basis_copy] + num_copies + w_copies:
        copy.wait_send()
    for k, copy in enumerate(fw_copies):
        owner_only(source(k), copy.wait)


def output_kernel(
    n, fresh, ag_in, fw_in, new_loadings, new_basis, nb, io_sem
):
    rank, pixels = nb.shape
    half, per, row_split = layout(n, rank, pixels)
    owners = half // per * row_split
    rows = rank // row_split
    me = lax.axis_index("scan")
    first_copy = pltpu.make_async_copy(fresh, new_loadings, io_sem.at[0])
    first_copy.start()

    def put(index, ref, flip):
        first, row = piece_at(index, per, row_split, rows)
        for j in range(per):
            block = first.start + j
            value = ref[j]
            if flip:
                block = pixels // LANES - 1 - block
                value = mirrored(value)
            nb[row, pl.ds(pl.multiple_of(block * LANES, LANES), LANES)] = value

    copies = []
    for flip, ref in enumerate((ag_in, fw_in)):
        for k in range(n):
            index = lax.rem(me + n - k, n)

            def go():
                put(index, ref.at[k], flip)

            if owners == n:
                go()
            else:
                pl.when(index < owners)(go)
        part = pl.ds(flip * (pixels // 2), pixels // 2)
        copies.append(
            pltpu.make_async_copy(nb.at[:, part], new_basis.at[:, part], io_sem.at[1 + flip])
        )
        copies[flip].start()
    first_copy.wait()
    for copy in copies:
        copy.wait()


def per_device(n, spectra, basis, loadings):
    rank, pixels = basis.shape
    positions = loadings.shape[1]
    blocks = pixels // LANES
    half, per, row_split = layout(n, rank, pixels)
    rows = rank // row_split
    slots = 1 if half // per * row_split == n else n
    chunk = positions // 8
    pos_chunk = positions // 4
    col_chunk = 4 * LANES
    pack = LANES // rank
    dma = pltpu.SemaphoreType.DMA
    any_space = pl.BlockSpec(memory_space=pl.ANY)
    vmem = pl.BlockSpec(memory_space=pltpu.VMEM)
    hbm = pl.BlockSpec(memory_space=pltpu.HBM)
    inputs = [pltpu.with_memory_space_constraint(x, pltpu.HBM) for x in (spectra, basis, loadings)]
    outs = pl.pallas_call(
        functools.partial(update_kernel, n, chunk, 4, 4, pos_chunk, col_chunk),
        out_shape=(
            pltpu.VMEM(loadings.shape, F32),
            pltpu.VMEM((n, per, rows, LANES), F32),
            pltpu.VMEM((n, per, rows, LANES), F32),
        ),
        in_specs=[hbm] * 3,
        out_specs=(vmem,) * 3,
        scratch_shapes=[
            pltpu.VMEM(spectra.shape, F32),
            pltpu.VMEM(spectra.shape, BF16),
            pltpu.VMEM(spectra.shape, BF16),
            pltpu.VMEM((rank, pixels), F32),
            pltpu.VMEM((rank, pixels), F32),
            pltpu.VMEM((blocks, rank, LANES), F32),
            pltpu.VMEM((2 * rank, pixels), BF16),
            pltpu.VMEM((rank, positions), F32),
            pltpu.VMEM((rank, positions), F32),
            pltpu.VMEM((2 * rank, positions), BF16),
            pltpu.VMEM((positions // pos_chunk, rank, pos_chunk), F32),
            pltpu.VMEM((positions // pos_chunk, rank, pos_chunk), F32),
            pltpu.VMEM((half, rank, LANES), F32),
            pltpu.VMEM((half, rank, LANES), F32),
            pltpu.VMEM((half, rank, LANES), F32),
            pltpu.VMEM((n, per, rows, LANES), F32),
            pltpu.VMEM((rank // pack, LANES), F32),
            pltpu.VMEM((n, rank // pack, LANES), F32),
            pltpu.SemaphoreType.REGULAR,
            pltpu.SemaphoreType.REGULAR,
            dma((positions // 2 // chunk + 1,)),
            dma((2,)),
            dma((2,)),
            dma((2, 2)),
            dma((2, half * LANES // col_chunk)),
            dma((slots,)), dma((slots,)), dma((1,)), dma((1,)),
            dma((slots,)), dma((max(slots, 2),)), dma((max(slots, 2),)), dma((max(slots, 2),)),
        ],
        compiler_params=pltpu.CompilerParams(
            collective_id=0, has_side_effects=True, vmem_limit_bytes=40 << 20
        ),
        name="update",
    )(*inputs)
    return pl.pallas_call(
        functools.partial(output_kernel, n),
        out_shape=(
            jax.ShapeDtypeStruct(loadings.shape, F32),
            jax.ShapeDtypeStruct(basis.shape, F32),
        ),
        in_specs=[vmem] * 3,
        out_specs=(any_space,) * 2,
        scratch_shapes=[pltpu.VMEM((rank, pixels), F32), dma((3,))],
        compiler_params=pltpu.CompilerParams(vmem_limit_bytes=8 << 20),
        name="write_out",
    )(*outs)


def solution(mesh):
    in_specs = (P(("grp", "scan"), "det"), P("grp", "det"), P("grp", "scan"))
    out_specs = (P("grp", "scan"), P("grp", "det"))
    return jax.shard_map(
        functools.partial(per_device, mesh.shape["scan"]),
        mesh=mesh, in_specs=in_specs, out_specs=out_specs, check_vma=False,
    )
```

```python
import functools

import jax
import jax.numpy as jnp
from jax import lax
from jax.experimental import pallas as pl
from jax.experimental.pallas import tpu as pltpu
from jax.sharding import PartitionSpec as P

HIGHEST = lax.Precision.HIGHEST
MESH = pl.DeviceIdType.MESH
F32 = jnp.float32
BF16 = jnp.bfloat16
LANES = 128


def split(x):
    hi = x.astype(BF16)
    lo = (x - hi.astype(F32)).astype(BF16)
    return hi, lo


def dot_nt(a, b):
    return lax.dot_general(a, b, (((1,), (1,)), ((), ())), preferred_element_type=F32)


def dot_nn(a, b):
    return lax.dot_general(a, b, (((1,), (0,)), ((), ())), preferred_element_type=F32)


def product(a, b):
    a_hi, a_lo = split(a)
    b_hi, b_lo = split(b)
    return dot_nn(a_hi, b_hi) + (dot_nn(a_hi, b_lo) + dot_nn(a_lo, b_hi))


def mirrored(x):
    index = (LANES - 1) - lax.broadcasted_iota(jnp.int32, x.shape, 1)
    return jnp.take_along_axis(x, index, axis=1, mode="promise_in_bounds")


def remote(src, dst, send, recv, where):
    return pltpu.make_async_remote_copy(
        src_ref=src, dst_ref=dst, send_sem=send, recv_sem=recv,
        device_id=where, device_id_type=MESH,
    )


def layout(n, rank, pixels):
    half = pixels // LANES // 2
    if n <= half:
        per, row_split = half // n, 1
    else:
        per, row_split = 1, min(n // half, rank // 8)
    return half, per, row_split


def piece_at(index, per, row_split, rows):
    first = index // row_split * per
    row = pl.multiple_of(lax.rem(index, row_split) * rows, 8) if row_split > 1 else 0
    return pl.ds(first, per), pl.ds(row, rows)


def divide(source, s_hi, s_lo, start, rows):
    @pl.loop(0, rows // 16, unroll=True)
    def _(j):
        part = pl.ds(pl.multiple_of(start + j * 16, 16), 16)
        hi, lo = split(source[part, :])
        s_hi[part, :] = hi
        s_lo[part, :] = lo


def update_kernel(
    n, chunk, early, flight, pos_chunk, col_chunk,
    spectra, basis, loadings,
    new_loadings, ag_in, fw_in,
    sbuf, s_hi, s_lo, own, other, tied3, tied2, load, weighted,
    nl2, num_out, num_in, w_keep, w_out, w_in, rs_in, cr_out, cr_in,
    hello, ready, sp_sem, io_sem, bs_sem,
    nm_sem, w_sem, rs_send, rs_recv, cr_send, cr_recv,
    ag_send, ag_recv, fw_send, fw_recv,
):
    blocks, rank, _ = tied3.shape
    half, per, row_split = layout(n, rank, blocks * LANES)
    owners = half // per * row_split
    rows = rank // row_split
    pack = LANES // rank
    me = lax.axis_index("scan")
    det = lax.axis_index("det")
    partner = {"det": 1 - det}
    positions = load.shape[1]
    first_rows = positions // 2
    first_chunks = first_rows // chunk
    single = owners == n
    middle = max(n // 2, 1)

    def peer(k):
        return lax.rem(me + k, n)

    def source(k):
        return lax.rem(me + n - k, n)

    def slot(k):
        return 0 if single else k

    def group(buffer, send, recv):
        part = pl.ds(1, n - 1)
        return remote(buffer.at[part], buffer.at[part], send.at[0], recv.at[0], partner)

    def owner_only(index, fn):
        if owners == n:
            fn()
        else:
            pl.when(index < owners)(fn)

    barrier = pltpu.get_barrier_semaphore()

    @pl.when(det == 0)
    def _():
        pl.semaphore_signal(barrier, inc=1, device_id=partner, device_id_type=MESH)

    spectra_copies = []
    for i in range(positions // chunk):
        part = pl.ds(i * chunk, chunk)
        spectra_copies.append(
            pltpu.make_async_copy(
                spectra.at[part], sbuf.at[part], sp_sem.at[min(i, first_chunks)]
            )
        )
    late_part = pl.ds(first_rows, positions - first_rows)
    late_copy = pltpu.make_async_copy(
        spectra.at[late_part], sbuf.at[late_part], sp_sem.at[first_chunks]
    )
    own_copy = pltpu.make_async_copy(basis, own, io_sem.at[0])
    load_copy = pltpu.make_async_copy(loadings, load, io_sem.at[1])
    basis_copy = remote(basis, other, bs_sem.at[0], bs_sem.at[1], partner)
    for i in range(early):
        spectra_copies[i].start()

    @pl.when(det == 1)
    def _():
        pl.semaphore_wait(barrier, 1)
        pl.semaphore_signal(hello, inc=1, device_id=partner, device_id_type=MESH)
        basis_copy.start()

    @pl.when(det == 0)
    def _():
        pl.semaphore_wait(hello, 1)
        basis_copy.start()
        for k in range(1, n):
            pl.semaphore_signal(
                barrier, inc=1, device_id={"scan": peer(k)}, device_id_type=MESH
            )

    own_copy.start()
    load_copy.start()
    for i in range(early, flight):
        spectra_copies[i].start()

    for i in range(first_chunks):
        spectra_copies[i].wait()
        if i + flight < len(spectra_copies):
            spectra_copies[i + flight].start()
        divide(sbuf, s_hi, s_lo, i * chunk, chunk)
    own_copy.wait()
    basis_copy.wait_recv()
    for b in range(blocks):
        mine = own[:, b * LANES:(b + 1) * LANES]
        back = blocks - 1 - b
        tied = 0.5 * (mine + mirrored(other[:, back * LANES:(back + 1) * LANES]))
        tied3[b] = tied
        hi, lo = split(tied)
        tied2[:rank, b * LANES:(b + 1) * LANES] = hi
        tied2[rank:, b * LANES:(b + 1) * LANES] = lo
    load_copy.wait()

    chunks = positions // pos_chunk
    num_copies = []
    for i in range(2):
        part = pl.ds(i * (chunks // 2), chunks // 2)
        num_copies.append(
            remote(num_out.at[part], num_in.at[part], nm_sem.at[0, i], nm_sem.at[1, i], partner)
        )

    def products(start):
        part = slice(start, start + chunk)
        both = dot_nt(s_hi[part, :], tied2[...])
        low = dot_nt(s_lo[part, :], tied2[:rank, :])
        at = start % pos_chunk
        num_out[start // pos_chunk, :, at:at + chunk] = (
            both[:, :rank] + (both[:, rank:] + low)
        ).T

    for i in range(first_chunks + flight, len(spectra_copies)):
        spectra_copies[i].start()
    for i in range(first_chunks):
        products(i * chunk)
    num_copies[0].start()
    late_copy.wait()
    divide(sbuf, s_hi, s_lo, first_rows, chunk)
    for i in range(first_chunks, positions // chunk):
        if (i + 1) * chunk < positions:
            divide(sbuf, s_hi, s_lo, (i + 1) * chunk, chunk)
        products(i * chunk)
        if i == first_chunks:
            squares = dot_nt(tied2[...], tied2[...])
            gram = 2.0 * (
                squares[:rank, :rank] + (squares[:rank, rank:] + squares[rank:, :rank])
            )
            weighted[...] = product(gram, load[...])
    num_copies[1].start()

    def update(i):
        cols = slice(i * pos_chunk, (i + 1) * pos_chunk)
        fresh = load[:, cols] * (num_out[i] + num_in[i]) / weighted[:, cols]
        new_loadings[:, cols] = fresh
        hi, lo = split(fresh)
        nl2[:rank, cols] = hi
        nl2[rank:, cols] = lo

    def sums(cols, where):
        both = dot_nn(nl2[:, where], s_hi[where, cols])
        low = dot_nn(nl2[:rank, where], s_lo[where, cols])
        return both[:rank] + (both[rank:] + low)

    step = col_chunk // LANES
    count = half // step

    def accumulate(target, first, i, where, add):
        start = first + i * step
        value = sums(slice(start * LANES, (start + step) * LANES), where)
        for j in range(step):
            at = value[:, j * LANES:(j + 1) * LANES]
            target[i * step + j] = target[i * step + j] + at if add else at

    w_copies = []
    for i in range(count):
        part = pl.ds(i * step, step)
        w_copies.append(
            remote(w_out.at[part], w_in.at[part], w_sem.at[0, i], w_sem.at[1, i], partner)
        )
    early_rows, late_rows = slice(0, first_rows), slice(first_rows, positions)
    num_copies[0].wait_recv()
    for i in range(chunks // 2):
        update(i)
    for i in range(count):
        accumulate(w_out, half, i, early_rows, False)
    for i in range(count):
        accumulate(w_keep, 0, i, early_rows, False)

    @pl.when(det == 0)
    def _():
        pl.semaphore_wait(barrier, n - 1)
        pl.semaphore_signal(ready, inc=1, device_id=partner, device_id_type=MESH)

    num_copies[1].wait_recv()
    for i in range(chunks // 2, chunks):
        update(i)
    for i in range(count):
        accumulate(w_out, half, i, late_rows, True)
        w_copies[i].start()

    @pl.when(det == 1)
    def _():
        pl.semaphore_wait(ready, 1)

    cr_copies = [None]
    for k in range(1, n):
        cr_copies.append(
            remote(cr_out, cr_in.at[k], cr_send.at[0], cr_recv.at[0], {"scan": peer(k)})
        )
    squares = dot_nt(nl2[...], nl2[...])
    cross = squares[:rank, :rank] + (squares[:rank, rank:] + squares[rank:, :rank])
    cr_out[...] = jnp.concatenate(
        [cross[i * (rank // pack):(i + 1) * (rank // pack)] for i in range(pack)], axis=1
    )
    for k in range(1, n):
        cr_copies[k].start()

    for i in range(count):
        accumulate(w_keep, 0, i, late_rows, True)

    rs_copies = [None]
    for k in range(1, n):
        rs_copies.append(
            remote(
                w_keep.at[piece_at(peer(k), per, row_split, rows)], rs_in.at[k],
                rs_send.at[slot(k)], rs_recv.at[slot(k)], {"scan": peer(k)},
            )
        )
    for i in range(count):
        w_copies[i].wait_recv()
        for j in range(step):
            b = half - 1 - (i * step + j)
            w_keep[b] = w_keep[b] + mirrored(w_in[half - 1 - b])
        if step % per:
            low, high = (0, half) if i == count - 1 else (0, 0)
        else:
            low, high = half - (i + 1) * step, half - i * step
        for k in range(1, n):
            first = peer(k) // row_split * per
            pl.when((first >= low) & (first < high))(rs_copies[k].start)

    group(cr_in, cr_send, cr_recv).wait_recv()
    total = cr_out[...]
    for k in range(1, n):
        total = total + cr_in[k]
    cross = jnp.concatenate(
        [total[:, i * rank:(i + 1) * rank] for i in range(pack)], axis=0
    )

    piece_buf = ag_in.at[0]
    ag_copies = [None]
    for k in range(1, n):
        ag_copies.append(
            remote(piece_buf, ag_in.at[k], ag_send.at[slot(k)], ag_recv.at[k // middle if single else k], {"scan": peer(k)})
        )
    if single:
        parts = [(low, min(low + middle, n)) for low in range(0, n, middle)]
        fw_copies = []
        for i, (low, high) in enumerate(parts):
            part = pl.ds(low, high - low)
            fw_copies.append(
                remote(ag_in.at[part], fw_in.at[part], fw_send.at[i], fw_recv.at[i], partner)
            )
    else:
        fw_copies = [
            remote(ag_in.at[k], fw_in.at[k], fw_send.at[k], fw_recv.at[k], partner)
            for k in range(n)
        ]

    def own_piece():
        first, row = piece_at(me, per, row_split, rows)
        for j in range(per):
            weights = jnp.dot(
                cross, tied3[first.start + j], precision=HIGHEST, preferred_element_type=F32
            )
            if row_split > 1:
                piece_buf[0] = weights[:rows]
                for i in range(1, row_split):
                    @pl.when(lax.rem(me, row_split) == i)
                    def _():
                        piece_buf[0] = weights[i * rows:(i + 1) * rows]
            else:
                piece_buf[j] = weights
        if single:
            group(rs_in, rs_send, rs_recv).wait_recv()
        else:
            for k in range(1, n):
                rs_copies[k].wait_recv()
        for j in range(per):
            total = w_keep[first.start + j, row, :]
            for k in range(1, n):
                total = total + rs_in[k, j]
            piece_buf[j] = tied3[first.start + j, row, :] * (0.5 * total) / piece_buf[j]
        for k in range(1, n):
            ag_copies[k].start()
        if not single:
            fw_copies[0].start()

    owner_only(me, own_piece)

    def arrived(k):
        def go():
            ag_copies[k].wait_recv()
            fw_copies[k].start()
        return go

    if single:
        for i, (low, high) in reversed(list(enumerate(parts))):
            part = pl.ds(max(low, 1), high - max(low, 1))
            if high > max(low, 1):
                remote(
                    ag_in.at[part], ag_in.at[part], ag_send.at[0], ag_recv.at[i], partner
                ).wait_recv()
            fw_copies[i].start()
        group(rs_in, rs_send, rs_recv).wait_send()
        group(ag_in, ag_send, ag_recv).wait_send()
    else:
        for k in range(1, n):
            owner_only(source(k), arrived(k))
        for k in range(1, n):
            owner_only(peer(k), rs_copies[k].wait_send)
            owner_only(me, ag_copies[k].wait_send)
    group(cr_in, cr_send, cr_recv).wait_send()
    for copy in [basis_copy] + num_copies + w_copies:
        copy.wait_send()
    for k, copy in enumerate(fw_copies):
        owner_only(source(k), copy.wait)


def output_kernel(
    n, fresh, ag_in, fw_in, new_loadings, new_basis, nb, io_sem
):
    rank, pixels = nb.shape
    half, per, row_split = layout(n, rank, pixels)
    owners = half // per * row_split
    rows = rank // row_split
    me = lax.axis_index("scan")
    first_copy = pltpu.make_async_copy(fresh, new_loadings, io_sem.at[0])
    first_copy.start()

    def put(index, ref, flip):
        first, row = piece_at(index, per, row_split, rows)
        for j in range(per):
            block = first.start + j
            value = ref[j]
            if flip:
                block = pixels // LANES - 1 - block
                value = mirrored(value)
            nb[row, pl.ds(pl.multiple_of(block * LANES, LANES), LANES)] = value

    copies = []
    for flip, ref in enumerate((ag_in, fw_in)):
        for k in range(n):
            index = lax.rem(me + n - k, n)

            def go():
                put(index, ref.at[k], flip)

            if owners == n:
                go()
            else:
                pl.when(index < owners)(go)
        part = pl.ds(flip * (pixels // 2), pixels // 2)
        copies.append(
            pltpu.make_async_copy(nb.at[:, part], new_basis.at[:, part], io_sem.at[1 + flip])
        )
        copies[flip].start()
    first_copy.wait()
    for copy in copies:
        copy.wait()


def per_device(n, spectra, basis, loadings):
    rank, pixels = basis.shape
    positions = loadings.shape[1]
    blocks = pixels // LANES
    half, per, row_split = layout(n, rank, pixels)
    rows = rank // row_split
    slots = 1 if half // per * row_split == n else n
    chunk = positions // 8
    pos_chunk = positions // 4
    col_chunk = 4 * LANES
    pack = LANES // rank
    dma = pltpu.SemaphoreType.DMA
    any_space = pl.BlockSpec(memory_space=pl.ANY)
    vmem = pl.BlockSpec(memory_space=pltpu.VMEM)
    hbm = pl.BlockSpec(memory_space=pltpu.HBM)
    inputs = [pltpu.with_memory_space_constraint(x, pltpu.HBM) for x in (spectra, basis, loadings)]
    outs = pl.pallas_call(
        functools.partial(update_kernel, n, chunk, 4, 4, pos_chunk, col_chunk),
        out_shape=(
            pltpu.VMEM(loadings.shape, F32),
            pltpu.VMEM((n, per, rows, LANES), F32),
            pltpu.VMEM((n, per, rows, LANES), F32),
        ),
        in_specs=[hbm] * 3,
        out_specs=(vmem,) * 3,
        scratch_shapes=[
            pltpu.VMEM(spectra.shape, F32),
            pltpu.VMEM(spectra.shape, BF16),
            pltpu.VMEM(spectra.shape, BF16),
            pltpu.VMEM((rank, pixels), F32),
            pltpu.VMEM((rank, pixels), F32),
            pltpu.VMEM((blocks, rank, LANES), F32),
            pltpu.VMEM((2 * rank, pixels), BF16),
            pltpu.VMEM((rank, positions), F32),
            pltpu.VMEM((rank, positions), F32),
            pltpu.VMEM((2 * rank, positions), BF16),
            pltpu.VMEM((positions // pos_chunk, rank, pos_chunk), F32),
            pltpu.VMEM((positions // pos_chunk, rank, pos_chunk), F32),
            pltpu.VMEM((half, rank, LANES), F32),
            pltpu.VMEM((half, rank, LANES), F32),
            pltpu.VMEM((half, rank, LANES), F32),
            pltpu.VMEM((n, per, rows, LANES), F32),
            pltpu.VMEM((rank // pack, LANES), F32),
            pltpu.VMEM((n, rank // pack, LANES), F32),
            pltpu.SemaphoreType.REGULAR,
            pltpu.SemaphoreType.REGULAR,
            dma((positions // 2 // chunk + 1,)),
            dma((2,)),
            dma((2,)),
            dma((2, 2)),
            dma((2, half * LANES // col_chunk)),
            dma((slots,)), dma((slots,)), dma((1,)), dma((1,)),
            dma((slots,)), dma((max(slots, 2),)), dma((max(slots, 2),)), dma((max(slots, 2),)),
        ],
        compiler_params=pltpu.CompilerParams(
            collective_id=0, has_side_effects=True, vmem_limit_bytes=40 << 20
        ),
        name="update",
    )(*inputs)
    return pl.pallas_call(
        functools.partial(output_kernel, n),
        out_shape=(
            jax.ShapeDtypeStruct(loadings.shape, F32),
            jax.ShapeDtypeStruct(basis.shape, F32),
        ),
        in_specs=[vmem] * 3,
        out_specs=(any_space,) * 2,
        scratch_shapes=[pltpu.VMEM((rank, pixels), F32), dma((3,))],
        compiler_params=pltpu.CompilerParams(vmem_limit_bytes=8 << 20),
        name="write_out",
    )(*outs)


def solution(mesh):
    in_specs = (P(("grp", "scan"), "det"), P("grp", "det"), P("grp", "scan"))
    out_specs = (P("grp", "scan"), P("grp", "det"))
    return jax.shard_map(
        functools.partial(per_device, mesh.shape["scan"]),
        mesh=mesh, in_specs=in_specs, out_specs=out_specs, check_vma=False,
    )
```
